32 devices in a mesh: grp: 2 (over x), gz: 16 (over z, y, core).
Axes of the slice: x: 2, y: 2, z: 4, core: 2. Of those that a mesh axis runs over, the one named last changes fastest.
Arguments:
- features: bfloat16 [12, 128, 32, 128], P(None, ('grp', 'gz')), parts along dimension 1, may hold values from -6 to 6
- w_first: bfloat16 [48, 324], replicated, may hold values from -0.5 to 0.5
- w_second: bfloat16 [96, 1296], replicated, may hold values from -0.25 to 0.25
- w_lift: bfloat16 [48, 96], replicated, may hold values from -0.875 to 0.875
- w_merge: bfloat16 [12, 1296], replicated, may hold values from -0.15625 to 0.15625
- w_affine: bfloat16 [3, 12], replicated, may hold values from -2.5 to 2.5
- tissue: int32 [32, 32], P(('grp', 'gz')), parts along dimension 0, may hold values from 0 to 31, as said below
- owners: int32 [32, 32], P(('grp', 'gz')), parts along dimension 0, may hold values from 0 to 15, as said below
Outputs:
- routed: bfloat16 [32, 16, 2, 1536], P(('grp', 'gz')), parts along dimension 0
The draws below stay inside these ranges and needn't reach their ends.
There are 2 independent parts, one for each index of `grp`. The reference program is written for one: setup_inputs(seed, part) draws one part's arguments, and reference() takes and returns one part's arrays. A program takes and returns all parts, laid end to end along the dimension named above; an argument that names none is the same for every part. Nothing has to cross between parts.
Inputs may be any that keep to these rules, and one draw needn't show every extreme that they name: `tissue`: each row lists 32 different blocks of that device, numbered as in the reference program. `owners`: A device sends at most 2 of its listed blocks to one owner; in every draw some owner receives exactly 2 from every device.
All inputs are finite; a program needn't handle non-finite values.
Results may differ from the reference program's by a relative error of at most 0.0054.
Values may be sent and summed in bfloat16 or wider, within the bound.
No kernel may reach another device: no remote copies, remote signals or barrier semaphores. Data moves between devices by JAX's collectives and lax.ppermute only.
A program may use at most 128 MiB of HBM per device.

```python
import jax
import jax.numpy as jnp
from jax import lax

C0 = 12
C1 = 48
C2 = 96
CU = 12
AFF = 3
ZD = 4
NY = 32
NX = 128
BY = 8
BX = 16
TISSUE = 32
SEND_CAP = 2
SLOTS = 32
NZ = 64
NB = 32
TILE = 1536
N_GZ = 16


def draw_tissue(key, part):

    def one_row(source):
        return jax.random.permutation(jax.random.fold_in(key, source), NB)[:TISSUE].astype(jnp.int32)
    return jax.vmap(one_row)(jnp.arange(N_GZ))


def draw_owners(key, part):
    hottest = jax.random.randint(jax.random.fold_in(key, 11), (), 0, N_GZ)
    others = (hottest + 1 + jnp.arange(N_GZ - 1)) % N_GZ
    stocked = jnp.tile(others, SEND_CAP).astype(jnp.int32)

    def one_row(source):
        row_key = jax.random.fold_in(jax.random.fold_in(key, 23), source)
        rest = jax.random.permutation(row_key, stocked)[:TISSUE - SEND_CAP]
        whole = jnp.concatenate([jnp.full((SEND_CAP,), hottest, jnp.int32), rest.astype(jnp.int32)])
        return jax.random.permutation(jax.random.fold_in(row_key, 7), whole).astype(jnp.int32)
    return jax.vmap(one_row)(jnp.arange(N_GZ))


def levels(own_key, shape, pieces, low, high):
    factor_of, own = 1.0, jax.random.fold_in(own_key, 6)
    for dim, parts in pieces:
        draws = jnp.exp(jax.random.uniform(jax.random.fold_in(own, dim), (parts,), jnp.float32, low / len(pieces), high / len(pieces)))
        factor_of = factor_of * jnp.repeat(draws, shape[dim] // parts).reshape([-1 if axis == dim else 1 for axis in range(len(shape))])
    return factor_of


def scatter_about(key, dims, width, most, cuts=(), held_as=jnp.bfloat16):
    loudness = levels(key, dims, cuts, -0.22, 0.18) if cuts else 1.0
    entries = jax.random.normal(key, dims, jnp.float32) * width * loudness
    return jnp.minimum(jnp.maximum(entries, -most), most).astype(held_as)


def setup_inputs(seed: int = 0, part: int = 0) -> dict:
    key_list = jax.random.split(jax.random.key(seed), 9)
    part_keys = jax.random.split(jax.random.fold_in(key_list[8], part), 9)
    features = scatter_about(part_keys[0], (C0, NZ, NY, NX), 1.0, 6.0, ((1, 16),))
    w_first = scatter_about(key_list[1], (C1, 27 * C0), (27 * C0 // 2) ** -0.5, 0.5)
    w_second = scatter_about(key_list[2], (C2, 27 * C1), (27 * C1 // 2) ** -0.5, 0.25)
    w_lift = scatter_about(key_list[3], (C1, C2), (C2 // 2) ** -0.5, 0.875)
    w_merge = scatter_about(key_list[4], (CU, 27 * C1), (27 * C1) ** -0.5, 0.15625)
    w_affine = scatter_about(key_list[5], (AFF, CU), (CU // 2) ** -0.5, 2.5)
    tissue = draw_tissue(jax.random.fold_in(jax.random.fold_in(key_list[8], part), 71), part)
    owners = draw_owners(jax.random.fold_in(jax.random.fold_in(key_list[8], part), 71), part)
    return dict(features=features, w_first=w_first, w_second=w_second, w_lift=w_lift, w_merge=w_merge, w_affine=w_affine, tissue=tissue, owners=owners)


def convolve(volume, weight, depth_pad):
    kernel = weight.reshape(weight.shape[0], 3, 3, 3, volume.shape[0]).transpose(0, 4, 1, 2, 3)
    result = lax.conv_general_dilated(volume[None], kernel, (1, 1, 1), [(depth_pad, depth_pad), (1, 1), (1, 1)], dimension_numbers=("NCDHW", "OIDHW", "NCDHW"), preferred_element_type=jnp.float32)
    return result[0]


def maxpool(volume):
    shape = volume.shape
    return volume.reshape(shape[0], shape[1] // 2, 2, shape[2] // 2, 2, shape[3] // 2, 2).max(axis=(2, 4, 6))


def upsample(volume):
    shape = volume.shape
    spread = jnp.broadcast_to(volume[:, :, None, :, None, :, None], (shape[0], shape[1], 2, shape[2], 2, shape[3], 2))
    return spread.reshape(shape[0], 2 * shape[1], 2 * shape[2], 2 * shape[3])


def reference(features, w_first, w_second, w_lift, w_merge, w_affine, tissue, owners):
    first_map = jax.nn.relu(convolve(features, w_first, 1)).astype(jnp.bfloat16)
    pooled = maxpool(first_map)
    second_map = jax.nn.relu(convolve(pooled, w_second, 1)).astype(jnp.bfloat16)
    lifted = jnp.einsum("oc,czyx->ozyx", w_lift.astype(jnp.float32), second_map.astype(jnp.float32))
    merged = (upsample(lifted) + first_map.astype(jnp.float32)).astype(jnp.bfloat16)
    third_map = jax.nn.relu(convolve(merged, w_merge, 1))
    affinity = jax.nn.sigmoid(jnp.einsum("ac,czyx->azyx", w_affine.astype(jnp.float32), third_map, precision=lax.Precision.HIGHEST)).astype(jnp.bfloat16)
    tiles = affinity.reshape(AFF, N_GZ, ZD, NY // BY, BY, NX // BX, BX).transpose(1, 3, 5, 0, 2, 4, 6).reshape(N_GZ, NB, TILE)
    same_owner = owners[:, :, None] == owners[:, None, :]
    earlier = jnp.arange(TISSUE)[None, :] < jnp.arange(TISSUE)[:, None]
    ranks = jnp.sum(same_owner & earlier[None], axis=2).astype(jnp.int32)
    slot_index = owners * SEND_CAP + ranks
    slot_pick = (slot_index[:, :, None] == jnp.arange(SLOTS, dtype=jnp.int32)[None, None, :]).astype(jnp.float32)
    block_pick = (tissue[:, :, None] == jnp.arange(NB, dtype=jnp.int32)[None, None, :]).astype(jnp.float32)
    select = jnp.einsum("skt,skb->stb", slot_pick, block_pick)
    outgoing = jnp.einsum("stb,sbe->ste", select, tiles.astype(jnp.float32))
    routed = outgoing.reshape(N_GZ, N_GZ, SEND_CAP, TILE).transpose(1, 0, 2, 3)
    return routed.astype(jnp.bfloat16)
```

```python
import functools

import jax
import jax.numpy as jnp
from jax import lax
from jax.experimental import pallas as pl
from jax.experimental.pallas import tpu as pltpu
from jax.sharding import PartitionSpec as P

BY = 8
BX = 16
SEND_CAP = 2
HALO = 3
F32 = jnp.float32
BF16 = jnp.bfloat16


def iota(shape, dim):
    return lax.broadcasted_iota(jnp.int32, shape, dim)


def beside(value, width):
    lane = iota(value.shape, 1) % width
    left = jnp.where(lane == 0, jnp.zeros_like(value), pltpu.roll(value, 1, 1))
    right = jnp.where(
        lane == width - 1, jnp.zeros_like(value), pltpu.roll(value, value.shape[1] - 1, 1)
    )
    return left, value, right


def trunk_kernel(
    flags,
    features,
    from_pair,
    from_next,
    w_first,
    w_second,
    w_lift,
    w_merge,
    inner,
    to_pair,
    to_next,
    plain,
    cols_1,
    first,
    cols_2,
    cols_3,
    total,
    edge,
):
    c0, depth, rows, lanes = features.shape
    c1 = w_lift.shape[0]
    c2 = w_lift.shape[1]
    half_rows = rows // 2
    wide = depth + 2 * HALO
    odd = flags[0]
    low_ok = flags[1]
    high_ok = flags[2]

    for z in range(HALO):
        for c in range(c0):
            a = from_pair[c, z].astype(F32)
            b = from_next[c, z].astype(F32)
            plain[z, c] = jnp.where(odd == 1, a, b)
            plain[HALO + depth + z, c] = jnp.where(odd == 1, b, a)
    for z in range(depth):
        for c in range(c0):
            plain[HALO + z, c] = features[c, z].astype(F32)

    pad_1 = jnp.zeros((cols_1.shape[2], lanes), BF16)
    for z in range(wide):
        cols_1[z, 0] = pad_1
        cols_1[z, rows + 1] = pad_1

    gap = jnp.zeros((16 - c0, lanes), F32)

    def spread_1(z, carry):
        flat = plain.at[z].reshape(c0 * rows, lanes)
        for y in range(rows):
            face = flat[pl.ds(y, c0, stride=rows), :]
            face = jnp.concatenate([face, gap], axis=0)
            cols_1[z, y + 1] = jnp.concatenate(beside(face, lanes), axis=0).astype(BF16)
        return carry

    lax.fori_loop(0, wide, spread_1, 0)

    weight_1 = w_first[...]
    run_1 = 16

    def conv_1(i, carry):
        z = i // (rows // run_1)
        y = (i % (rows // run_1)) * run_1
        x = jnp.concatenate(
            [
                jnp.concatenate(
                    [cols_1[z + a, y + b + j] for a in range(3) for b in range(3)], axis=0
                )
                for j in range(run_1)
            ],
            axis=1,
        )
        out = jnp.dot(weight_1, x, preferred_element_type=F32)
        out = jnp.maximum(out, 0.0).astype(BF16)
        for j in range(run_1):
            first[z, y + j] = out[:, j * lanes : (j + 1) * lanes]
        return carry

    lax.fori_loop(0, (wide - 2) * (rows // run_1), conv_1, 0)

    pick = (iota((2 * lanes, lanes), 0) == 2 * iota((2 * lanes, lanes), 1)).astype(BF16)
    lane = iota((c1, lanes), 1)
    low_half = lane < lanes // 2
    keep_low = jnp.logical_or(jnp.logical_not(low_half), low_ok == 1)
    keep_high = jnp.logical_or(low_half, high_ok == 1)
    pad_2 = jnp.zeros((3 * c1, lanes), BF16)
    for a in range(3):
        cols_2[a, 0] = pad_2
        cols_2[a, half_rows + 1] = pad_2

    def pool(y, carry):
        tops = []
        for p in range(4):
            m = jnp.maximum(
                jnp.maximum(first[2 * p, 2 * y], first[2 * p, 2 * y + 1]),
                jnp.maximum(first[2 * p + 1, 2 * y], first[2 * p + 1, 2 * y + 1]),
            ).astype(F32)
            tops.append(jnp.maximum(m, pltpu.roll(m, lanes - 1, 1)).astype(BF16))
        both = jnp.concatenate(
            [
                jnp.concatenate([tops[0], tops[1]], axis=1),
                jnp.concatenate([tops[2], tops[3]], axis=1),
            ],
            axis=0,
        )
        packed = jnp.dot(both, pick, preferred_element_type=F32)
        low = jnp.where(keep_low, packed[:c1], 0.0)
        high = jnp.where(keep_high, packed[c1:], 0.0)
        middle = pltpu.roll(jnp.where(low_half, high, low), lanes // 2, 1)
        for a, value in enumerate((low, middle, high)):
            cols_2[a, y + 1] = jnp.concatenate(beside(value, lanes // 2), axis=0).astype(BF16)
        return carry

    lax.fori_loop(0, half_rows, pool, 0)

    weight_2 = w_second[...]
    weight_l = w_lift[...]
    widen = (iota((lanes, 2 * lanes), 0) == iota((lanes, 2 * lanes), 1) // 2).astype(BF16)
    run_2 = 4

    def conv_2(i, carry):
        y = i * run_2
        x = jnp.concatenate(
            [
                jnp.concatenate(
                    [cols_2[a, y + b + j] for a in range(3) for b in range(3)], axis=0
                )
                for j in range(run_2)
            ],
            axis=1,
        )
        second = jnp.dot(weight_2, x, preferred_element_type=F32)
        second = jnp.maximum(second, 0.0).astype(BF16)
        stacked = jnp.concatenate(
            [second[:, j * lanes : (j + 1) * lanes] for j in range(run_2)], axis=0
        )
        stacked = jnp.dot(stacked, widen, preferred_element_type=F32).astype(BF16)
        spread = jnp.concatenate(
            [stacked[j * c2 : (j + 1) * c2] for j in range(run_2)], axis=1
        )
        lifted = jnp.dot(weight_l, spread, preferred_element_type=F32)
        for j in range(run_2):
            for zz in range(2):
                at = (2 * j + zz) * lanes
                value = lifted[:, at : at + lanes]
                for dz in range(2):
                    for dy in range(2):
                        z = 2 * zz + dz
                        row = 2 * (y + j) + dy
                        merged = value + first[z + 2, row].astype(F32)
                        merged = merged.astype(BF16).astype(F32)
                        cols_3[z, row] = jnp.concatenate(beside(merged, lanes), axis=0).astype(
                            BF16
                        )
        return carry

    lax.fori_loop(0, half_rows // run_2, conv_2, 0)

    total[...] = jnp.zeros_like(total)
    weight_3 = w_merge[...]
    run_3 = 8

    def conv_3(i, carry):
        z = i // (rows // run_3)
        y = (i % (rows // run_3)) * run_3
        x = jnp.concatenate([cols_3[z, y + j] for j in range(run_3)], axis=1)
        out = jnp.dot(weight_3, x, preferred_element_type=F32)
        for a in range(3):
            for k in range(run_3 + 2):
                term = None
                for b in range(3):
                    j = k - 2 + b
                    if 0 <= j < run_3:
                        at = (a * 3 + b) * 16
                        value = out[at : at + 16, j * lanes : (j + 1) * lanes]
                        term = value if term is None else term + value
                total[z + 2 - a, y + k] += term
        return carry

    lax.fori_loop(0, depth * (rows // run_3), conv_3, 0)

    cu = edge.shape[0] // rows
    for target, plane in ((to_pair, jnp.where(odd == 1, 0, depth + 1)),
                          (to_next, jnp.where(odd == 1, depth + 1, 0))):
        for y in range(rows):
            edge[y * cu : (y + 1) * cu] = total[plane, y + 1, 0:cu]
        target[...] = edge[...].astype(BF16)
    for z in range(depth):
        inner[z] = total[z + 1, 1 : rows + 1]


def tail_kernel(flags, inner, from_pair, from_next, w_head, tissue, owners, out, edge, shown):
    depth, rows, _, lanes = inner.shape
    cu = from_pair.shape[0] // rows
    odd = flags[0]
    a = from_pair[...].astype(F32)
    b = from_next[...].astype(F32)
    edge[0] = jnp.where(odd == 1, a, b)
    edge[1] = jnp.where(odd == 1, b, a)
    head = w_head[...]
    gap = jnp.zeros((16 - cu, lanes), F32)
    run = 8
    for y0 in range(0, rows, run):
        columns = []
        for y in range(y0, y0 + run):
            parts = []
            for z in range(depth):
                value = inner[z, y]
                if z == 0:
                    value = value + jnp.concatenate([edge[0, y * cu : (y + 1) * cu], gap], axis=0)
                if z == depth - 1:
                    value = value + jnp.concatenate([edge[1, y * cu : (y + 1) * cu], gap], axis=0)
                value = jnp.maximum(value, 0.0)
                for _ in range(3):
                    part = value.astype(BF16)
                    parts.append(part)
                    value = value - part.astype(F32)
            columns.append(jnp.concatenate(parts, axis=0))
        logits = jnp.dot(head, jnp.concatenate(columns, axis=1), preferred_element_type=F32)
        chance = jax.nn.sigmoid(logits)
        for j in range(run):
            shown[(y0 + j) * 16 : (y0 + j + 1) * 16] = chance[:, j * lanes : (j + 1) * lanes]

    sub = iota((BY, lanes), 0)
    group = iota((BY, lanes), 1) // BX
    faces = 3 * depth
    tiles = []
    for f in range(faces):
        blocks = []
        for by in range(rows // BY):
            v = shown[pl.ds(by * BY * 16 + f, BY, stride=16), :]
            for k in (1, 2, 4):
                s_bit = (sub // k) % 2
                g_bit = (group // k) % 2
                down = pltpu.roll(pltpu.roll(v, BY - k, 0), k * BX, 1)
                up = pltpu.roll(pltpu.roll(v, k, 0), lanes - k * BX, 1)
                v = jnp.where(s_bit == g_bit, v, jnp.where(s_bit < g_bit, down, up))
            blocks.append(v)
        tiles.append(jnp.concatenate(blocks, axis=0))
    tiles = jnp.concatenate(tiles, axis=1).astype(BF16)

    count = tissue.shape[1]
    slots = out.shape[0]
    own = jnp.broadcast_to(owners[...], (count, count))
    seen = jnp.broadcast_to(tissue[...], (count, count))
    r = iota((count, count), 0)
    c = iota((count, count), 1)
    own_column = jnp.sum(jnp.where(r == c, own, 0), axis=1, keepdims=True)
    seen_column = jnp.sum(jnp.where(r == c, seen, 0), axis=1, keepdims=True)
    before = jnp.where(jnp.logical_and(own_column == own, r < c), 1, 0)
    slot = owners[...] * SEND_CAP + jnp.sum(before, axis=0, keepdims=True)
    slot_pick = (iota((slots, count), 0) == slot).astype(F32).astype(BF16)
    blocks = tiles.shape[0]
    block_pick = (seen_column == iota((count, blocks), 1)).astype(F32).astype(BF16)
    select = jnp.dot(slot_pick, block_pick, preferred_element_type=F32).astype(BF16)
    out[...] = jnp.dot(select, tiles, preferred_element_type=F32).astype(BF16)


def on_device(features, w_first, w_second, w_lift, w_merge, w_affine, tissue, owners):
    c0, depth, rows, lanes = features.shape
    c1, c2 = w_lift.shape
    cu = w_merge.shape[0]
    devices = lax.axis_size("gz")
    here = lax.axis_index("gz")
    odd = here % 2
    flags = jnp.stack([odd, (here > 0).astype(jnp.int32), (here < devices - 1).astype(jnp.int32)])
    pair = [(i, i ^ 1) for i in range(devices)]
    after = [(i, i + 1) for i in range(1, devices - 1, 2)]
    after = after + [(j, i) for i, j in after]

    lower = lax.slice_in_dim(features, 0, HALO, axis=1)
    upper = lax.slice_in_dim(features, depth - HALO, depth, axis=1)
    from_next = lax.ppermute(jnp.where(odd == 1, upper, lower), "gz", after)
    from_pair = lax.ppermute(jnp.where(odd == 1, lower, upper), "gz", pair)

    first_cols = jnp.pad(w_first.reshape(c1, 27, c0), ((0, 0), (0, 0), (0, 16 - c0)))
    first_cols = first_cols.reshape(c1, 27 * 16)
    merge_rows = w_merge.reshape(cu, 9, 3 * c1).transpose(1, 0, 2)
    merge_rows = jnp.pad(merge_rows, ((0, 0), (0, 16 - cu), (0, 0))).reshape(9 * 16, 3 * c1)
    head = jnp.pad(w_affine, ((0, 0), (0, 16 - cu)))
    head = jnp.tile(head, (1, 3))
    head = jnp.einsum("ac,zw->azwc", head, jnp.eye(depth, dtype=head.dtype))
    head = jnp.pad(head.reshape(3 * depth, -1), ((0, 16 - 3 * depth), (0, 0)))

    vmem = pl.BlockSpec(memory_space=pltpu.VMEM)
    smem = pl.BlockSpec(memory_space=pltpu.SMEM)
    shape = jax.ShapeDtypeStruct
    wide = depth + 2 * HALO
    inner, to_pair, to_next = pl.pallas_call(
        trunk_kernel,
        out_shape=(
            shape((depth, rows, 16, lanes), F32),
            shape((rows * cu, lanes), BF16),
            shape((rows * cu, lanes), BF16),
        ),
        in_specs=[smem] + [vmem] * 7,
        out_specs=(vmem,) * 3,
        scratch_shapes=[
            pltpu.VMEM((wide, c0, rows, lanes), F32),
            pltpu.VMEM((wide, rows + 2, 48, lanes), BF16),
            pltpu.VMEM((wide - 2, rows, c1, lanes), BF16),
            pltpu.VMEM((3, rows // 2 + 2, 3 * c1, lanes), BF16),
            pltpu.VMEM((depth, rows, 3 * c1, lanes), BF16),
            pltpu.VMEM((depth + 2, rows + 2, 16, lanes), F32),
            pltpu.VMEM((rows * cu, lanes), F32),
        ],
        name="trunk",
    )(flags, features, from_pair, from_next, first_cols, w_second, w_lift, merge_rows)

    edge_next = lax.ppermute(to_next, "gz", after)
    edge_pair = lax.ppermute(to_pair, "gz", pair)
    outgoing = pl.pallas_call(
        tail_kernel,
        out_shape=shape((devices * SEND_CAP, 3 * depth * BY * BX), BF16),
        in_specs=[smem] + [vmem] * 6,
        out_specs=vmem,
        scratch_shapes=[
            pltpu.VMEM((2, rows * cu, lanes), F32),
            pltpu.VMEM((rows * 16, lanes), F32),
        ],
        name="tail",
    )(flags, inner, edge_pair, edge_next, head, tissue, owners)
    outgoing = outgoing.reshape(devices, SEND_CAP, -1)
    return lax.all_to_all(outgoing, "gz", split_axis=0, concat_axis=0, tiled=True)[None]


def solution(mesh):
    placed = (
        P(None, ("grp", "gz"), None, None),
        P(),
        P(),
        P(),
        P(),
        P(),
        P(("grp", "gz"), None),
        P(("grp", "gz"), None),
    )
    return jax.shard_map(
        on_device,
        mesh=mesh,
        in_specs=placed,
        out_specs=P(("grp", "gz"), None, None, None),
        check_vma=False,
    )
```

```python
import jax
import jax.numpy as jnp
import numpy as np
from jax import lax
from jax.experimental import pallas as pl
from jax.experimental.pallas import tpu as pltpu
from jax.sharding import PartitionSpec as P

BY = 8
BX = 16
SEND_CAP = 2
HALO = 3
F32 = jnp.float32
BF16 = jnp.bfloat16


def iota(shape, dim):
    return lax.broadcasted_iota(jnp.int32, shape, dim)


def beside(value, width):
    lane = iota(value.shape, 1) % width
    left = jnp.where(lane == 0, jnp.zeros_like(value), pltpu.roll(value, 1, 1))
    right = jnp.where(
        lane == width - 1, jnp.zeros_like(value), pltpu.roll(value, value.shape[1] - 1, 1)
    )
    return left, value, right


def trunk_kernel(
    flags,
    features,
    from_pair,
    from_next,
    w_first,
    w_second,
    w_lift,
    w_edge,
    to_pair,
    to_next,
    cols_3,
    plain,
    cols_1,
    first,
    cols_2,
    border,
    edge,
):
    c0, depth, rows, lanes = features.shape
    c1, c2 = w_lift.shape
    half_rows = rows // 2
    wide = depth + 2 * HALO
    pairs = (wide - 2) // 2
    odd = flags[0]
    low_ok = flags[1]
    high_ok = flags[2]

    def face_at(z, c):
        return slice((z * c0 + c) * rows, (z * c0 + c + 1) * rows)

    for z in range(HALO):
        for c in range(c0):
            a = from_pair[c, z].astype(F32)
            b = from_next[c, z].astype(F32)
            plain[face_at(z, c)] = jnp.where(odd == 1, a, b)
            plain[face_at(HALO + depth + z, c)] = jnp.where(odd == 1, b, a)
    for z in range(depth):
        for c in range(c0):
            plain[face_at(HALO + z, c)] = features[c, z].astype(F32)

    group = 4 * c0
    pad_1 = jnp.zeros((3 * group, lanes), BF16)
    for p in range(pairs):
        cols_1[p, 0] = pad_1
        cols_1[p, rows + 1] = pad_1

    def spread_1(p, carry):
        for y in range(rows):
            face = plain[pl.ds(p * (2 * c0 * rows) + y, group, stride=rows), :]
            cols_1[p, y + 1] = jnp.concatenate(beside(face, lanes), axis=0).astype(BF16)
        return carry

    lax.fori_loop(0, pairs, spread_1, 0)

    weight_1 = w_first[...]
    run_1 = 16

    def conv_1(i, carry):
        p = i // (rows // run_1)
        y = (i % (rows // run_1)) * run_1
        x = jnp.concatenate(
            [
                jnp.concatenate([cols_1[p, y + b + j] for b in range(3)], axis=0)
                for j in range(run_1)
            ],
            axis=1,
        )
        out = jnp.dot(weight_1, x, preferred_element_type=F32)
        out = jnp.maximum(out, 0.0).astype(BF16)
        for j in range(run_1):
            for z in range(2):
                first[2 * p + z, y + j] = out[z * c1 : (z + 1) * c1, j * lanes : (j + 1) * lanes]
        return carry

    lax.fori_loop(0, pairs * (rows // run_1), conv_1, 0)

    pick = (iota((2 * lanes, lanes), 0) == 2 * iota((2 * lanes, lanes), 1)).astype(BF16)
    lane = iota((c1, lanes), 1)
    low_half = lane < lanes // 2
    keep_low = jnp.logical_or(jnp.logical_not(low_half), low_ok == 1)
    keep_high = jnp.logical_or(low_half, high_ok == 1)
    pad_2 = jnp.zeros((3 * c1, lanes), BF16)
    for a in range(3):
        cols_2[a, 0] = pad_2
        cols_2[a, half_rows + 1] = pad_2
    run_p = 4

    def pool(i, carry):
        y0 = i * run_p
        both = []
        for j in range(run_p):
            y = 2 * (y0 + j)
            tops = []
            for p in range(4):
                m = jnp.maximum(
                    jnp.maximum(first[2 * p, y], first[2 * p, y + 1]),
                    jnp.maximum(first[2 * p + 1, y], first[2 * p + 1, y + 1]),
                ).astype(F32)
                tops.append(jnp.maximum(m, pltpu.roll(m, lanes - 1, 1)).astype(BF16))
            both.append(jnp.concatenate([tops[0], tops[1]], axis=1))
            both.append(jnp.concatenate([tops[2], tops[3]], axis=1))
        packed = jnp.dot(jnp.concatenate(both, axis=0), pick, preferred_element_type=F32)
        for j in range(run_p):
            at = 2 * j * c1
            low = jnp.where(keep_low, packed[at : at + c1], 0.0)
            high = jnp.where(keep_high, packed[at + c1 : at + 2 * c1], 0.0)
            middle = pltpu.roll(jnp.where(low_half, high, low), lanes // 2, 1)
            for a, value in enumerate((low, middle, high)):
                value = jnp.concatenate(beside(value, lanes // 2), axis=0)
                cols_2[a, y0 + j + 1] = value.astype(BF16)
        return carry

    lax.fori_loop(0, half_rows // run_p, pool, 0)

    weight_2 = w_second[...]
    weight_l = w_lift[...]
    widen = (iota((lanes, 2 * lanes), 0) == iota((lanes, 2 * lanes), 1) // 2).astype(BF16)
    run_2 = 4

    def conv_2(i, carry):
        y = i * run_2
        x = jnp.concatenate(
            [
                jnp.concatenate(
                    [cols_2[a, y + b + j] for a in range(3) for b in range(3)], axis=0
                )
                for j in range(run_2)
            ],
            axis=1,
        )
        second = jnp.dot(weight_2, x, preferred_element_type=F32)
        second = jnp.maximum(second, 0.0).astype(BF16)
        stacked = jnp.concatenate(
            [second[:, j * lanes : (j + 1) * lanes] for j in range(run_2)], axis=0
        )
        stacked = jnp.dot(stacked, widen, preferred_element_type=F32).astype(BF16)
        spread = jnp.concatenate(
            [stacked[j * c2 : (j + 1) * c2] for j in range(run_2)], axis=1
        )
        lifted = jnp.dot(weight_l, spread, preferred_element_type=F32)
        for j in range(run_2):
            for zz in range(2):
                at = (2 * j + zz) * lanes
                value = lifted[:, at : at + lanes]
                for dz in range(2):
                    for dy in range(2):
                        z = 2 * zz + dz
                        row = 2 * (y + j) + dy
                        merged = value + first[z + 2, row].astype(F32)
                        merged = merged.astype(BF16).astype(F32)
                        cols_3[z, row] = jnp.concatenate(beside(merged, lanes), axis=0).astype(
                            BF16
                        )
        return carry

    lax.fori_loop(0, half_rows // run_2, conv_2, 0)

    cu = edge.shape[0] // rows
    border[...] = jnp.zeros_like(border)
    weight_e = w_edge[...]
    run_e = 8

    def conv_e(i, carry):
        y = i * run_e
        x = jnp.concatenate(
            [
                jnp.concatenate([cols_3[0, y + j], cols_3[depth - 1, y + j]], axis=0)
                for j in range(run_e)
            ],
            axis=1,
        )
        out = jnp.dot(weight_e, x, preferred_element_type=F32)
        for k, term in row_sums(out, run_e, 2 * cu, lanes):
            border[y + k] += term
        return carry

    lax.fori_loop(0, rows // run_e, conv_e, 0)

    for target, upward in ((to_pair, odd == 0), (to_next, odd == 1)):
        for y in range(rows):
            down = border[y + 1, 0:cu]
            up = border[y + 1, cu : 2 * cu]
            edge[y * cu : (y + 1) * cu] = jnp.where(upward, up, down)
        target[...] = edge[...].astype(BF16)


def row_sums(out, run, height, lanes):
    for k in range(run + 2):
        term = None
        for b in range(3):
            j = k - 2 + b
            if 0 <= j < run:
                value = out[b * height : (b + 1) * height, j * lanes : (j + 1) * lanes]
                term = value if term is None else term + value
        yield k, term


def inner_kernel(cols_3, w_inner, inner):
    depth, rows, _, lanes = cols_3.shape
    height = inner.shape[2]
    run = 8
    for q in range(2):
        inner[q, 0] = jnp.zeros((height, lanes), F32)
        inner[q, 1] = jnp.zeros((height, lanes), F32)
        weight = w_inner[q]

        def conv_3(i, carry, q=q, weight=weight):
            y = i * run
            x = jnp.concatenate(
                [
                    jnp.concatenate([cols_3[q + a, y + j] for a in range(3)], axis=0)
                    for j in range(run)
                ],
                axis=1,
            )
            out = jnp.dot(weight, x, preferred_element_type=F32)
            for k, term in row_sums(out, run, height, lanes):
                if k < 2:
                    inner[q, y + k] += term
                else:
                    inner[q, y + k] = term
            return carry

        lax.fori_loop(0, rows // run, conv_3, 0)


def tail_kernel(flags, inner, from_pair, from_next, w_head, tissue, owners, out, edge, shown):
    depth = 4
    height, lanes = inner.shape[2:]
    rows = inner.shape[1] - 2
    cu = from_pair.shape[0] // rows
    odd = flags[0]
    a = from_pair[...].astype(F32)
    b = from_next[...].astype(F32)
    edge[0] = jnp.where(odd == 1, a, b)
    edge[1] = jnp.where(odd == 1, b, a)
    head = w_head[...]
    gap = jnp.zeros((height - cu, lanes), F32)
    run = 8
    for y0 in range(0, rows, run):
        columns = []
        for y in range(y0, y0 + run):
            parts = []
            value = jnp.concatenate(
                [
                    inner[q, y + 1]
                    + jnp.concatenate([edge[q, y * cu : (y + 1) * cu], gap], axis=0)
                    for q in range(2)
                ],
                axis=0,
            )
            value = jnp.maximum(value, 0.0)
            for _ in range(3):
                part = value.astype(BF16)
                parts.append(part)
                value = value - part.astype(F32)
            columns.append(jnp.concatenate(parts, axis=0))
        logits = jnp.dot(head, jnp.concatenate(columns, axis=1), preferred_element_type=F32)
        chance = jax.nn.sigmoid(logits)
        for j in range(run):
            shown[(y0 + j) * 16 : (y0 + j + 1) * 16] = chance[:, j * lanes : (j + 1) * lanes]

    sub = iota((BY, lanes), 0)
    group = iota((BY, lanes), 1) // BX
    faces = 3 * depth
    tiles = []
    for f in range(faces):
        blocks = []
        for by in range(rows // BY):
            v = shown[pl.ds(by * BY * 16 + f, BY, stride=16), :]
            for k in (1, 2, 4):
                s_bit = (sub // k) % 2
                g_bit = (group // k) % 2
                down = pltpu.roll(pltpu.roll(v, BY - k, 0), k * BX, 1)
                up = pltpu.roll(pltpu.roll(v, k, 0), lanes - k * BX, 1)
                v = jnp.where(s_bit == g_bit, v, jnp.where(s_bit < g_bit, down, up))
            blocks.append(v)
        tiles.append(jnp.concatenate(blocks, axis=0))
    tiles = jnp.concatenate(tiles, axis=1).astype(BF16)

    count = tissue.shape[1]
    slots = out.shape[0]
    own = jnp.broadcast_to(owners[...], (count, count))
    seen = jnp.broadcast_to(tissue[...], (count, count))
    r = iota((count, count), 0)
    c = iota((count, count), 1)
    own_column = jnp.sum(jnp.where(r == c, own, 0), axis=1, keepdims=True)
    seen_column = jnp.sum(jnp.where(r == c, seen, 0), axis=1, keepdims=True)
    before = jnp.where(jnp.logical_and(own_column == own, r < c), 1, 0)
    slot = owners[...] * SEND_CAP + jnp.sum(before, axis=0, keepdims=True)
    slot_pick = (iota((slots, count), 0) == slot).astype(F32).astype(BF16)
    blocks = tiles.shape[0]
    block_pick = (seen_column == iota((count, blocks), 1)).astype(F32).astype(BF16)
    select = jnp.dot(slot_pick, block_pick, preferred_element_type=F32).astype(BF16)
    out[...] = jnp.dot(select, tiles, preferred_element_type=F32).astype(BF16)


def on_device(features, w_first, w_second, w_lift, w_merge, w_affine, tissue, owners):
    c0, depth, rows, lanes = features.shape
    c1, c2 = w_lift.shape
    cu = w_merge.shape[0]
    devices = lax.axis_size("gz")
    here = lax.axis_index("gz")
    odd = here % 2
    flags = jnp.stack([odd, (here > 0).astype(jnp.int32), (here < devices - 1).astype(jnp.int32)])
    pair = [(i, i ^ 1) for i in range(devices)]
    after = [(i, i + 1) for i in range(1, devices - 1, 2)]
    after = after + [(j, i) for i, j in after]

    lower = lax.slice_in_dim(features, 0, HALO, axis=1)
    upper = lax.slice_in_dim(features, depth - HALO, depth, axis=1)
    from_next = lax.ppermute(jnp.where(odd == 1, upper, lower), "gz", after)
    from_pair = lax.ppermute(jnp.where(odd == 1, lower, upper), "gz", pair)

    taps = w_first.reshape(c1, 3, 3, 3, c0).transpose(0, 2, 3, 1, 4)
    taps = jnp.stack(
        [jnp.pad(taps, ((0, 0),) * 3 + ((z, 1 - z), (0, 0))) for z in range(2)]
    ).reshape(2 * c1, 36 * c0)

    merge = w_merge.reshape(cu, 3, 3, 3 * c1).transpose(1, 2, 0, 3)
    none = jnp.zeros_like(merge[0])

    def arrange(table):
        table = [[none if a is None else merge[a] for a in line] for line in table]
        whole = jnp.stack([jnp.concatenate(line, axis=2) for line in table], axis=1)
        return whole.reshape(3 * len(table) * cu, -1)

    w_edge = arrange([[2, None], [None, 0]])
    w_inner = jnp.stack(
        [arrange([[1, 2, None], [0, 1, 2]]), arrange([[None, 0, 1], [0, 1, 2]])]
    )
    place = jnp.asarray(np.eye(4)[:, [0, 1, 3, 2]], w_affine.dtype)
    head = w_affine[:, None, None, :] * place[None, :, :, None]
    head = jnp.tile(head.reshape(3 * depth, depth * cu), (1, 3))
    head = jnp.pad(head, ((0, 16 - 3 * depth), (0, 0)))
    taps, w_edge, w_inner, head = lax.optimization_barrier((taps, w_edge, w_inner, head))

    vmem = pl.BlockSpec(memory_space=pltpu.VMEM)
    smem = pl.BlockSpec(memory_space=pltpu.SMEM)
    shape = jax.ShapeDtypeStruct
    wide = depth + 2 * HALO
    to_pair, to_next, cols_3 = pl.pallas_call(
        trunk_kernel,
        out_shape=(
            shape((rows * cu, lanes), BF16),
            shape((rows * cu, lanes), BF16),
            shape((depth, rows, 3 * c1, lanes), BF16),
        ),
        in_specs=[smem] + [vmem] * 7,
        out_specs=(vmem,) * 3,
        scratch_shapes=[
            pltpu.VMEM((wide * c0 * rows, lanes), F32),
            pltpu.VMEM((wide // 2 - 1, rows + 2, 12 * c0, lanes), BF16),
            pltpu.VMEM((wide - 2, rows, c1, lanes), BF16),
            pltpu.VMEM((3, rows // 2 + 2, 3 * c1, lanes), BF16),
            pltpu.VMEM((rows + 2, 2 * cu, lanes), F32),
            pltpu.VMEM((rows * cu, lanes), F32),
        ],
        compiler_params=pltpu.CompilerParams(vmem_limit_bytes=24 * 2**20),
        name="trunk",
    )(flags, features, from_pair, from_next, taps, w_second, w_lift, w_edge)

    edge_next = lax.ppermute(to_next, "gz", after)
    edge_pair = lax.ppermute(to_pair, "gz", pair)
    inner = pl.pallas_call(
        inner_kernel,
        out_shape=shape((2, rows + 2, 2 * cu, lanes), F32),
        in_specs=[vmem] * 2,
        out_specs=vmem,
        compiler_params=pltpu.CompilerParams(vmem_limit_bytes=16 * 2**20),
        cost_estimate=pl.CostEstimate(
            flops=2 * 27 * c1 * cu * depth * rows * lanes,
            bytes_accessed=8 * 2**20,
            transcendentals=0,
        ),
        name="inner",
    )(cols_3, w_inner)
    outgoing = pl.pallas_call(
        tail_kernel,
        out_shape=shape((devices * SEND_CAP, 3 * depth * BY * BX), BF16),
        in_specs=[smem] + [vmem] * 6,
        out_specs=vmem,
        scratch_shapes=[
            pltpu.VMEM((2, rows * cu, lanes), F32),
            pltpu.VMEM((rows * 16, lanes), F32),
        ],
        compiler_params=pltpu.CompilerParams(vmem_limit_bytes=8 * 2**20),
        name="tail",
    )(flags, inner, edge_pair, edge_next, head, tissue, owners)
    outgoing = outgoing.reshape(devices, SEND_CAP, -1)
    return lax.all_to_all(outgoing, "gz", split_axis=0, concat_axis=0, tiled=True)[None]


def solution(mesh):
    placed = (
        P(None, ("grp", "gz"), None, None),
        P(),
        P(),
        P(),
        P(),
        P(),
        P(("grp", "gz"), None),
        P(("grp", "gz"), None),
    )
    return jax.shard_map(
        on_device,
        mesh=mesh,
        in_specs=placed,
        out_specs=P(("grp", "gz"), None, None, None),
        check_vma=False,
    )
```

```python
import jax
import jax.numpy as jnp
import numpy as np
from jax import lax
from jax.experimental import pallas as pl
from jax.experimental.pallas import tpu as pltpu
from jax.sharding import PartitionSpec as P

BY = 8
BX = 16
SEND_CAP = 2
HALO = 3
F32 = jnp.float32
BF16 = jnp.bfloat16


def iota(shape, dim):
    return lax.broadcasted_iota(jnp.int32, shape, dim)


def beside(value, width):
    lane = iota(value.shape, 1) % width
    left = jnp.where(lane == 0, jnp.zeros_like(value), pltpu.roll(value, 1, 1))
    right = jnp.where(
        lane == width - 1, jnp.zeros_like(value), pltpu.roll(value, value.shape[1] - 1, 1)
    )
    return left, value, right


def trunk_kernel(
    flags,
    features,
    from_pair,
    from_next,
    w_first,
    w_second,
    w_lift,
    w_edge,
    to_pair,
    to_next,
    cols_3,
    plain,
    cols_1,
    first,
    cols_2,
    border,
    edge,
):
    c0, depth, rows, lanes = features.shape
    c1, c2 = w_lift.shape
    half_rows = rows // 2
    wide = depth + 2 * HALO
    pairs = (wide - 2) // 2
    odd = flags[0]
    low_ok = flags[1]
    high_ok = flags[2]

    pitch = plain.shape[0] // (wide * c0)
    def face_at(z, c):
        return slice((z * c0 + c) * pitch, (z * c0 + c) * pitch + rows)

    for z in range(HALO):
        for c in range(c0):
            a = from_pair[c, z].astype(F32)
            b = from_next[c, z].astype(F32)
            plain[face_at(z, c)] = jnp.where(odd == 1, a, b)
            plain[face_at(HALO + depth + z, c)] = jnp.where(odd == 1, b, a)
    for z in range(depth):
        for c in range(c0):
            plain[face_at(HALO + z, c)] = features[c, z].astype(F32)

    group = 4 * c0
    pad_1 = jnp.zeros((3 * group, lanes), BF16)
    for p in range(pairs):
        cols_1[p, 0] = pad_1
        cols_1[p, rows + 1] = pad_1

    def spread_1(p, carry):
        for y in range(rows):
            face = plain[pl.ds(p * (2 * c0 * pitch) + y, group, stride=pitch), :]
            cols_1[p, y + 1] = jnp.concatenate(beside(face.astype(BF16), lanes), axis=0)
        return carry

    lax.fori_loop(0, pairs, spread_1, 0)

    weight_1 = w_first[...]
    run_1 = 16

    def conv_1(i, carry):
        p = i // (rows // run_1)
        y = (i % (rows // run_1)) * run_1
        x = jnp.concatenate(
            [
                jnp.concatenate([cols_1[p, y + b + j] for b in range(3)], axis=0)
                for j in range(run_1)
            ],
            axis=1,
        )
        out = jnp.dot(weight_1, x, preferred_element_type=F32)
        out = jnp.maximum(out, 0.0).astype(BF16)
        for j in range(run_1):
            for z in range(2):
                first[2 * p + z, y + j] = out[z * c1 : (z + 1) * c1, j * lanes : (j + 1) * lanes]
        return carry

    lax.fori_loop(0, pairs * (rows // run_1), conv_1, 0, unroll=4)

    pick = (iota((2 * lanes, lanes), 0) == 2 * iota((2 * lanes, lanes), 1)).astype(BF16)
    lane = iota((c1, lanes), 1)
    low_half = lane < lanes // 2
    keep_low = jnp.logical_or(jnp.logical_not(low_half), low_ok == 1)
    keep_high = jnp.logical_or(low_half, high_ok == 1)
    pad_2 = jnp.zeros((3 * c1, lanes), BF16)
    for a in range(3):
        cols_2[a, 0] = pad_2
        cols_2[a, half_rows + 1] = pad_2
    run_p = 4
    zero_2 = jnp.zeros((c1, lanes), BF16)

    def pool(i, carry):
        y0 = i * run_p
        both = []
        for j in range(run_p):
            y = 2 * (y0 + j)
            tops = []
            for p in range(4):
                m = jnp.maximum(
                    jnp.maximum(first[2 * p, y], first[2 * p, y + 1]),
                    jnp.maximum(first[2 * p + 1, y], first[2 * p + 1, y + 1]),
                )
                tops.append(jnp.maximum(m, pltpu.roll(m, lanes - 1, 1)))
            both.append(jnp.concatenate([tops[0], tops[1]], axis=1))
            both.append(jnp.concatenate([tops[2], tops[3]], axis=1))
        packed = jnp.dot(jnp.concatenate(both, axis=0), pick, preferred_element_type=F32).astype(BF16)
        for j in range(run_p):
            at = 2 * j * c1
            low = jnp.where(keep_low, packed[at : at + c1], zero_2)
            high = jnp.where(keep_high, packed[at + c1 : at + 2 * c1], zero_2)
            middle = pltpu.roll(jnp.where(low_half, high, low), lanes // 2, 1)
            for a, value in enumerate((low, middle, high)):
                cols_2[a, y0 + j + 1] = jnp.concatenate(beside(value, lanes // 2), axis=0)
        return carry

    lax.fori_loop(0, half_rows // run_p, pool, 0, unroll=4)

    weight_2 = w_second[...]
    weight_l = w_lift[...]
    widen = (iota((lanes, 2 * lanes), 0) == iota((lanes, 2 * lanes), 1) // 2).astype(BF16)
    run_2 = 4

    def conv_2(i, carry):
        y = i * run_2
        x = jnp.concatenate(
            [
                jnp.concatenate(
                    [cols_2[a, y + b + j] for a in range(3) for b in range(3)], axis=0
                )
                for j in range(run_2)
            ],
            axis=1,
        )
        second = jnp.dot(weight_2, x, preferred_element_type=F32)
        second = jnp.maximum(second, 0.0).astype(BF16)
        stacked = jnp.concatenate(
            [second[:, j * lanes : (j + 1) * lanes] for j in range(run_2)], axis=0
        )
        stacked = jnp.dot(stacked, widen, preferred_element_type=F32).astype(BF16)
        spread = jnp.concatenate(
            [stacked[j * c2 : (j + 1) * c2] for j in range(run_2)], axis=1
        )
        lifted = jnp.dot(weight_l, spread, preferred_element_type=F32)
        for j in range(run_2):
            for zz in range(2):
                at = (2 * j + zz) * lanes
                value = lifted[:, at : at + lanes]
                for dz in range(2):
                    for dy in range(2):
                        z = 2 * zz + dz
                        row = 2 * (y + j) + dy
                        merged = value + first[z + 2, row].astype(F32)
                        merged = merged.astype(BF16)
                        cols_3[z, row] = jnp.concatenate(beside(merged, lanes), axis=0)
        return carry

    lax.fori_loop(0, half_rows // run_2, conv_2, 0, unroll=4)

    cu = edge.shape[0] // rows
    border[...] = jnp.zeros_like(border)
    weight_e = w_edge[...]
    run_e = 8

    def conv_e(i, carry):
        y = i * run_e
        x = jnp.concatenate(
            [
                jnp.concatenate([cols_3[0, y + j], cols_3[depth - 1, y + j]], axis=0)
                for j in range(run_e)
            ],
            axis=1,
        )
        out = jnp.dot(weight_e, x, preferred_element_type=F32)
        for k, term in row_sums(out, run_e, 2 * cu, lanes):
            border[y + k] += term
        return carry

    lax.fori_loop(0, rows // run_e, conv_e, 0, unroll=4)

    for target, upward in ((to_pair, odd == 0), (to_next, odd == 1)):
        for y in range(rows):
            down = border[y + 1, 0:cu]
            up = border[y + 1, cu : 2 * cu]
            edge[y * cu : (y + 1) * cu] = jnp.where(upward, up, down)
        target[...] = edge[...].astype(BF16)


def row_sums(out, run, height, lanes):
    for k in range(run + 2):
        term = None
        for b in range(3):
            j = k - 2 + b
            if 0 <= j < run:
                value = out[b * height : (b + 1) * height, j * lanes : (j + 1) * lanes]
                term = value if term is None else term + value
        yield k, term


def inner_kernel(cols_3, w_inner, inner):
    depth, rows, _, lanes = cols_3.shape
    height = inner.shape[2]
    run = 8
    for q in range(2):
        inner[q, 0] = jnp.zeros((height, lanes), F32)
        inner[q, 1] = jnp.zeros((height, lanes), F32)
        weight = w_inner[q]

        def conv_3(i, carry, q=q, weight=weight):
            y = i * run
            x = jnp.concatenate(
                [
                    jnp.concatenate([cols_3[q + a, y + j] for a in range(3)], axis=0)
                    for j in range(run)
                ],
                axis=1,
            )
            out = jnp.dot(weight, x, preferred_element_type=F32)
            for k, term in row_sums(out, run, height, lanes):
                if k < 2:
                    inner[q, y + k] += term
                else:
                    inner[q, y + k] = term
            return carry

        lax.fori_loop(0, rows // run, conv_3, 0, unroll=4)


def tail_kernel(flags, inner, from_pair, from_next, w_head, tissue, owners, out, edge, shown):
    depth = 4
    height, lanes = inner.shape[2:]
    rows = inner.shape[1] - 2
    cu = from_pair.shape[0] // rows
    odd = flags[0]
    a = from_pair[...].astype(F32)
    b = from_next[...].astype(F32)
    edge[0] = jnp.where(odd == 1, a, b)
    edge[1] = jnp.where(odd == 1, b, a)
    head = w_head[...]
    gap = jnp.zeros((height - cu, lanes), F32)
    run = 8
    for y0 in range(0, rows, run):
        columns = []
        for y in range(y0, y0 + run):
            parts = []
            value = jnp.concatenate(
                [
                    inner[q, y + 1]
                    + jnp.concatenate([edge[q, y * cu : (y + 1) * cu], gap], axis=0)
                    for q in range(2)
                ],
                axis=0,
            )
            value = jnp.maximum(value, 0.0)
            for _ in range(3):
                part = value.astype(BF16)
                parts.append(part)
                value = value - part.astype(F32)
            columns.append(jnp.concatenate(parts, axis=0))
        logits = jnp.dot(head, jnp.concatenate(columns, axis=1), preferred_element_type=F32)
        chance = jax.nn.sigmoid(logits)
        for j in range(run):
            shown[(y0 + j) * 24 : (y0 + j) * 24 + 16] = chance[:, j * lanes : (j + 1) * lanes]

    sub = iota((BY, lanes), 0)
    group = iota((BY, lanes), 1) // BX
    faces = 3 * depth
    tiles = []
    for f in range(faces):
        blocks = []
        for by in range(rows // BY):
            v = shown[pl.ds(by * BY * 24 + f, BY, stride=24), :]
            for k in (1, 2, 4):
                s_bit = (sub // k) % 2
                g_bit = (group // k) % 2
                down = pltpu.roll(pltpu.roll(v, BY - k, 0), k * BX, 1)
                up = pltpu.roll(pltpu.roll(v, k, 0), lanes - k * BX, 1)
                v = jnp.where(s_bit == g_bit, v, jnp.where(s_bit < g_bit, down, up))
            blocks.append(v)
        tiles.append(jnp.concatenate(blocks, axis=0))
    tiles = jnp.concatenate(tiles, axis=1).astype(BF16)

    count = tissue.shape[1]
    slots = out.shape[0]
    own = jnp.broadcast_to(owners[...], (count, count))
    seen = jnp.broadcast_to(tissue[...], (count, count))
    r = iota((count, count), 0)
    c = iota((count, count), 1)
    own_column = jnp.sum(jnp.where(r == c, own, 0), axis=1, keepdims=True)
    seen_column = jnp.sum(jnp.where(r == c, seen, 0), axis=1, keepdims=True)
    before = jnp.where(jnp.logical_and(own_column == own, r < c), 1, 0)
    slot = owners[...] * SEND_CAP + jnp.sum(before, axis=0, keepdims=True)
    slot_pick = (iota((slots, count), 0) == slot).astype(F32).astype(BF16)
    blocks = tiles.shape[0]
    block_pick = (seen_column == iota((count, blocks), 1)).astype(F32).astype(BF16)
    select = jnp.dot(slot_pick, block_pick, preferred_element_type=F32).astype(BF16)
    out[...] = jnp.dot(select, tiles, preferred_element_type=F32).astype(BF16)


def on_device(features, w_first, w_second, w_lift, w_merge, w_affine, tissue, owners):
    c0, depth, rows, lanes = features.shape
    c1, c2 = w_lift.shape
    cu = w_merge.shape[0]
    devices = lax.axis_size("gz")
    here = lax.axis_index("gz")
    odd = here % 2
    flags = jnp.stack([odd, (here > 0).astype(jnp.int32), (here < devices - 1).astype(jnp.int32)])
    pair = [(i, i ^ 1) for i in range(devices)]
    after = [(i, i + 1) for i in range(1, devices - 1, 2)]
    after = after + [(j, i) for i, j in after]

    lower = lax.slice_in_dim(features, 0, HALO, axis=1)
    upper = lax.slice_in_dim(features, depth - HALO, depth, axis=1)
    from_next = lax.ppermute(jnp.where(odd == 1, upper, lower), "gz", after)
    from_pair = lax.ppermute(jnp.where(odd == 1, lower, upper), "gz", pair)

    taps = w_first.reshape(c1, 3, 3, 3, c0).transpose(0, 2, 3, 1, 4)
    taps = jnp.stack(
        [jnp.pad(taps, ((0, 0),) * 3 + ((z, 1 - z), (0, 0))) for z in range(2)]
    ).reshape(2 * c1, 36 * c0)

    merge = w_merge.reshape(cu, 3, 3, 3 * c1).transpose(1, 2, 0, 3)
    none = jnp.zeros_like(merge[0])

    def arrange(table):
        table = [[none if a is None else merge[a] for a in line] for line in table]
        whole = jnp.stack([jnp.concatenate(line, axis=2) for line in table], axis=1)
        return whole.reshape(3 * len(table) * cu, -1)

    w_edge = arrange([[2, None], [None, 0]])
    w_inner = jnp.stack(
        [arrange([[1, 2, None], [0, 1, 2]]), arrange([[None, 0, 1], [0, 1, 2]])]
    )
    place = jnp.asarray(np.eye(4)[:, [0, 1, 3, 2]], w_affine.dtype)
    head = w_affine[:, None, None, :] * place[None, :, :, None]
    head = jnp.tile(head.reshape(3 * depth, depth * cu), (1, 3))
    head = jnp.pad(head, ((0, 16 - 3 * depth), (0, 0)))
    taps, w_edge, w_inner, head = lax.optimization_barrier((taps, w_edge, w_inner, head))

    vmem = pl.BlockSpec(memory_space=pltpu.VMEM)
    smem = pl.BlockSpec(memory_space=pltpu.SMEM)
    shape = jax.ShapeDtypeStruct
    wide = depth + 2 * HALO
    to_pair, to_next, cols_3 = pl.pallas_call(
        trunk_kernel,
        out_shape=(
            shape((rows * cu, lanes), BF16),
            shape((rows * cu, lanes), BF16),
            shape((depth, rows, 3 * c1, lanes), BF16),
        ),
        in_specs=[smem] + [vmem] * 7,
        out_specs=(vmem,) * 3,
        scratch_shapes=[
            pltpu.VMEM((wide * c0 * (rows + 8), lanes), F32),
            pltpu.VMEM((wide // 2 - 1, rows + 2, 12 * c0, lanes), BF16),
            pltpu.VMEM((wide - 2, rows, c1, lanes), BF16),
            pltpu.VMEM((3, rows // 2 + 2, 3 * c1, lanes), BF16),
            pltpu.VMEM((rows + 2, 2 * cu, lanes), F32),
            pltpu.VMEM((rows * cu, lanes), F32),
        ],
        compiler_params=pltpu.CompilerParams(vmem_limit_bytes=24 * 2**20),
        name="trunk",
    )(flags, features, from_pair, from_next, taps, w_second, w_lift, w_edge)

    edge_next = lax.ppermute(to_next, "gz", after)
    edge_pair = lax.ppermute(to_pair, "gz", pair)
    inner = pl.pallas_call(
        inner_kernel,
        out_shape=shape((2, rows + 2, 2 * cu, lanes), F32),
        in_specs=[vmem] * 2,
        out_specs=vmem,
        compiler_params=pltpu.CompilerParams(vmem_limit_bytes=16 * 2**20),
        cost_estimate=pl.CostEstimate(
            flops=2 * 27 * c1 * cu * depth * rows * lanes,
            bytes_accessed=8 * 2**20,
            transcendentals=0,
        ),
        name="inner",
    )(cols_3, w_inner)
    outgoing = pl.pallas_call(
        tail_kernel,
        out_shape=shape((devices * SEND_CAP, 3 * depth * BY * BX), BF16),
        in_specs=[smem] + [vmem] * 6,
        out_specs=vmem,
        scratch_shapes=[
            pltpu.VMEM((2, rows * cu, lanes), F32),
            pltpu.VMEM((rows * 24, lanes), F32),
        ],
        compiler_params=pltpu.CompilerParams(vmem_limit_bytes=8 * 2**20),
        name="tail",
    )(flags, inner, edge_pair, edge_next, head, tissue, owners)
    outgoing = outgoing.reshape(devices, SEND_CAP, -1)
    return lax.all_to_all(outgoing, "gz", split_axis=0, concat_axis=0, tiled=True)[None]


def solution(mesh):
    placed = (
        P(None, ("grp", "gz"), None, None),
        P(),
        P(),
        P(),
        P(),
        P(),
        P(("grp", "gz"), None),
        P(("grp", "gz"), None),
    )
    return jax.shard_map(
        on_device,
        mesh=mesh,
        in_specs=placed,
        out_specs=P(("grp", "gz"), None, None, None),
        check_vma=False,
    )
```

```python
import jax
import jax.numpy as jnp
from jax import lax
from jax.experimental import pallas as pl
from jax.experimental.pallas import tpu as pltpu
from jax.sharding import PartitionSpec as P


BY = 8
BX = 16
SEND_CAP = 2
HALO = 2
F32 = jnp.float32
BF16 = jnp.bfloat16


def iota(shape, dim):
    return lax.broadcasted_iota(jnp.int32, shape, dim)


def beside(value, width):
    lane = iota(value.shape, 1) % width
    left = jnp.where(lane == 0, jnp.zeros_like(value), pltpu.roll(value, 1, 1))
    right = jnp.where(
        lane == width - 1, jnp.zeros_like(value), pltpu.roll(value, value.shape[1] - 1, 1)
    )
    return left, value, right


def neighbours():
    here = lax.axis_index("gz")
    return here % 2, here > 0, here < lax.axis_size("gz") - 1


def cut_kernel(features, *rest):
    *refs, sems = rest
    half = (len(refs) - 3) // 2
    weights, (to_pair, to_next, held), fetched = refs[:half], refs[half : half + 3], refs[half + 3 :]
    odd = lax.axis_index("gz") % 2
    depth = features.shape[1]
    top, bottom = depth - HALO, 0
    copies = [
        pltpu.make_async_copy(
            features.at[:, pl.ds(jnp.where(odd == 1, top, bottom), HALO)], to_next, sems.at[0]
        ),
        pltpu.make_async_copy(
            features.at[:, pl.ds(jnp.where(odd == 1, bottom, top), HALO)], to_pair, sems.at[1]
        ),
    ]
    for k, pair in enumerate(zip((features, *weights), (held, *fetched))):
        copies.append(pltpu.make_async_copy(*pair, sems.at[2 + k]))
    for copy in copies:
        copy.start()
    for copy in copies:
        copy.wait()


def spread(plain, cols, pitch, group, rows):
    blank = jnp.zeros((3 * group, plain.shape[1]), BF16)
    cols[0] = blank
    cols[rows + 1] = blank
    for y in range(rows):
        face = plain[pl.ds(y, group, stride=pitch), :].astype(BF16)
        cols[y + 1] = jnp.concatenate(beside(face, face.shape[1]), axis=0)


def convolve_pair(weight, cols, first, at, rows, c1):
    run = 16
    lanes = cols.shape[2]
    for y in range(0, rows, run):
        x = jnp.concatenate(
            [
                jnp.concatenate([cols[y + b + j] for b in range(3)], axis=0)
                for j in range(run)
            ],
            axis=1,
        )
        out = jnp.dot(weight, x, preferred_element_type=F32)
        out = jnp.maximum(out, 0.0).astype(BF16)
        for j in range(run):
            for z in range(2):
                first[at + z, y + j] = out[z * c1 : (z + 1) * c1, j * lanes : (j + 1) * lanes]


def crest(*faces):
    top = faces[0]
    for face in faces[1:]:
        top = jnp.maximum(top, face)
    return jnp.maximum(top, pltpu.roll(top, top.shape[1] - 1, 1))


def even_lanes(lanes):
    return (iota((2 * lanes, lanes), 0) == 2 * iota((2 * lanes, lanes), 1)).astype(BF16)


def local_kernel(w_first, features, taps, near, to_pair, to_next, plain, cols):
    c0, depth, rows, lanes = features.shape
    c1 = w_first.shape[0]
    odd, _, _ = neighbours()
    pitch = plain.shape[0] // (depth * c0)
    weight = w_first[...]
    blank = jnp.zeros((c1, c0), BF16)
    for o in range(2):
        line = []
        for b in range(3):
            for d in range(3):
                for z in range(4):
                    at = (((z - o) * 3 + b) * 3 + d) * c0
                    line.append(weight[:, at : at + c0] if 0 <= z - o < 3 else blank)
        taps[o * c1 : (o + 1) * c1] = jnp.concatenate(line, axis=1)
    for z in range(depth):
        for c in range(c0):
            at = (z * c0 + c) * pitch
            plain[at : at + rows] = features[c, z].astype(F32)
    spread(plain, cols, pitch, 4 * c0, rows)
    convolve_pair(taps[...], cols, near, 0, rows, c1)
    fold = rows // 4
    tops = []
    for z in range(2):
        for y in range(fold):
            tops.append(
                jnp.concatenate(
                    [
                        crest(near[z, 2 * k], near[z, 2 * k + 1])
                        for k in (y, y + fold)
                    ],
                    axis=1,
                )
            )
    packed = jnp.dot(
        jnp.concatenate(tops, axis=0), even_lanes(lanes), preferred_element_type=F32
    ).astype(BF16)
    for y in range(fold):
        down = packed[y * c1 : (y + 1) * c1]
        up = packed[(fold + y) * c1 : (fold + y + 1) * c1]
        to_pair[y] = jnp.where(odd == 1, down, up)
        to_next[y] = jnp.where(odd == 1, up, down)


def first_kernel(taps, features, from_pair, from_next, first, plain, cols):
    c0, depth, rows, _ = features.shape
    c1 = first.shape[2]
    odd, _, _ = neighbours()
    pitch = plain.shape[1] // (4 * c0)
    for z in range(2):
        for c in range(c0):
            at = (z * c0 + c) * pitch
            after = ((z + 2) * c0 + c) * pitch
            a = from_pair[c, z].astype(F32)
            b = from_next[c, z].astype(F32)
            plain[0, at : at + rows] = jnp.where(odd == 1, a, b)
            plain[1, after : after + rows] = jnp.where(odd == 1, b, a)
            plain[0, after : after + rows] = features[c, z].astype(F32)
            plain[1, at : at + rows] = features[c, depth - 2 + z].astype(F32)
    weight = taps[...]
    for g in range(2):
        spread(plain.at[g], cols.at[g], pitch, 4 * c0, rows)
        convolve_pair(weight, cols.at[g], first, 2 * g, rows, c1)


def trunk_kernel(
    first,
    near,
    from_pair,
    from_next,
    w_second,
    w_lift,
    w_edge,
    to_pair,
    to_next,
    cols_3,
    cols_2,
    border,
    edge,
):
    _, rows, c1, lanes = first.shape
    c2 = w_second.shape[0]
    depth = cols_3.shape[0]
    half_rows = rows // 2
    odd, low_ok, high_ok = neighbours()
    own = (first.at[1], near.at[0], near.at[1], first.at[2])

    pick = even_lanes(lanes)
    lane = iota((c1, lanes), 1)
    low_half = lane < lanes // 2
    keep_low = jnp.logical_or(jnp.logical_not(low_half), low_ok)
    keep_high = jnp.logical_or(low_half, high_ok)
    pad_2 = jnp.zeros((3 * c1, lanes), BF16)
    zero_2 = jnp.zeros((c1, lanes), BF16)
    for a in range(3):
        cols_2[a, 0] = pad_2
        cols_2[a, half_rows + 1] = pad_2
    run_p = 4
    fold = half_rows // 2
    for y0 in range(0, half_rows, run_p):
        both = []
        for k in range(y0, y0 + run_p):
            y = 2 * k
            both.append(
                jnp.concatenate(
                    [
                        crest(first[0, y], first[0, y + 1]),
                        crest(own[0][y], own[0][y + 1], own[1][y], own[1][y + 1]),
                    ],
                    axis=1,
                )
            )
            both.append(
                jnp.concatenate(
                    [
                        crest(own[2][y], own[2][y + 1], own[3][y], own[3][y + 1]),
                        crest(first[3, y], first[3, y + 1]),
                    ],
                    axis=1,
                )
            )
        packed = jnp.dot(
            jnp.concatenate(both, axis=0), pick, preferred_element_type=F32
        ).astype(BF16)
        for j in range(run_p):
            k = y0 + j
            at = 2 * j * c1
            a = from_pair[k % fold]
            b = from_next[k % fold]
            below = jnp.where(odd == 1, a, b)
            above = jnp.where(odd == 1, b, a)
            if k < fold:
                above = pltpu.roll(above, lanes // 2, 1)
            else:
                below = pltpu.roll(below, lanes // 2, 1)
            low = packed[at : at + c1]
            high = packed[at + c1 : at + 2 * c1]
            low = jnp.where(low_half, jnp.maximum(low, below), low)
            high = jnp.where(low_half, high, jnp.maximum(high, above))
            low = jnp.where(keep_low, low, zero_2)
            high = jnp.where(keep_high, high, zero_2)
            middle = pltpu.roll(jnp.where(low_half, high, low), lanes // 2, 1)
            for a, value in enumerate((low, middle, high)):
                cols_2[a, k + 1] = jnp.concatenate(beside(value, lanes // 2), axis=0)

    weight_2 = w_second[...]
    weight_l = w_lift[...]
    widen = (iota((lanes, 2 * lanes), 0) == iota((lanes, 2 * lanes), 1) // 2).astype(BF16)
    run_2 = 4

    def conv_2(i, carry):
        y = i * run_2
        x = jnp.concatenate(
            [
                jnp.concatenate(
                    [cols_2[a, y + b + j] for a in range(3) for b in range(3)], axis=0
                )
                for j in range(run_2)
            ],
            axis=1,
        )
        second = jnp.dot(weight_2, x, preferred_element_type=F32)
        second = jnp.maximum(second, 0.0).astype(BF16)
        stacked = jnp.concatenate(
            [second[:, j * lanes : (j + 1) * lanes] for j in range(run_2)], axis=0
        )
        stacked = jnp.dot(stacked, widen, preferred_element_type=F32).astype(BF16)
        spread = jnp.concatenate(
            [stacked[j * c2 : (j + 1) * c2] for j in range(run_2)], axis=1
        )
        lifted = jnp.dot(weight_l, spread, preferred_element_type=F32)
        for j in range(run_2):
            for zz in range(2):
                at = (2 * j + zz) * lanes
                value = lifted[:, at : at + lanes]
                for dz in range(2):
                    for dy in range(2):
                        z = 2 * zz + dz
                        row = 2 * (y + j) + dy
                        merged = value + own[z][row].astype(F32)
                        merged = merged.astype(BF16)
                        cols_3[z, row] = jnp.concatenate(beside(merged, lanes), axis=0)
        return carry

    lax.fori_loop(0, half_rows // run_2, conv_2, 0, unroll=4)

    cu = edge.shape[0] // rows
    border[...] = jnp.zeros_like(border)
    weight_e = w_edge[...]
    run_e = 8

    def conv_e(i, carry):
        y = i * run_e
        x = jnp.concatenate(
            [
                jnp.concatenate([cols_3[0, y + j], cols_3[depth - 1, y + j]], axis=0)
                for j in range(run_e)
            ],
            axis=1,
        )
        out = jnp.dot(weight_e, x, preferred_element_type=F32)
        for k, term in row_sums(out, run_e, 2 * cu, lanes):
            border[y + k] += term
        return carry

    lax.fori_loop(0, rows // run_e, conv_e, 0, unroll=4)

    for target, upward in ((to_pair, odd == 0), (to_next, odd == 1)):
        for y in range(rows):
            down = border[y + 1, 0:cu]
            up = border[y + 1, cu : 2 * cu]
            edge[y * cu : (y + 1) * cu] = jnp.where(upward, up, down)
        target[...] = edge[...].astype(BF16)


def weights_kernel(w_merge, w_affine, w_edge, w_inner, head):
    cu, width = w_merge.shape
    width = width // 9
    merge = w_merge[...].astype(F32)
    none = jnp.zeros((cu, width), F32)

    def arrange(table):
        lines = []
        for b in range(3):
            for line in table:
                pieces = [
                    none if a is None else merge[:, (a * 3 + b) * width : (a * 3 + b + 1) * width]
                    for a in line
                ]
                lines.append(jnp.concatenate(pieces, axis=1))
        return jnp.concatenate(lines, axis=0).astype(BF16)

    w_edge[...] = arrange([[2, None], [None, 0]])
    w_inner[0] = arrange([[1, 2, None], [0, 1, 2]])
    w_inner[1] = arrange([[None, 0, 1], [0, 1, 2]])

    affine = w_affine[...].astype(F32)
    blank = jnp.zeros_like(affine)
    lines = []
    for z in range(4):
        at = (0, 1, 3, 2).index(z)
        line = [affine if k == at else blank for k in range(4)]
        lines.append(jnp.concatenate(line * 3, axis=1))
    lines.append(jnp.zeros((16 - 4 * affine.shape[0], 12 * cu), F32))
    head[...] = jnp.concatenate(lines, axis=0).astype(BF16)


def row_sums(out, run, height, lanes):
    for k in range(run + 2):
        term = None
        for b in range(3):
            j = k - 2 + b
            if 0 <= j < run:
                value = out[b * height : (b + 1) * height, j * lanes : (j + 1) * lanes]
                term = value if term is None else term + value
        yield k, term


def inner_kernel(cols_3, w_inner, inner):
    _, rows, _, lanes = cols_3.shape
    height = inner.shape[2]
    run = 8
    for q in range(2):
        inner[q, 0] = jnp.zeros((height, lanes), F32)
        inner[q, 1] = jnp.zeros((height, lanes), F32)
        weight = w_inner[q]

        def conv_3(i, carry, q=q, weight=weight):
            y = i * run
            x = jnp.concatenate(
                [
                    jnp.concatenate([cols_3[q + a, y + j] for a in range(3)], axis=0)
                    for j in range(run)
                ],
                axis=1,
            )
            out = jnp.dot(weight, x, preferred_element_type=F32)
            for k, term in row_sums(out, run, height, lanes):
                if k < 2:
                    inner[q, y + k] += term
                else:
                    inner[q, y + k] = term
            return carry

        lax.fori_loop(0, rows // run, conv_3, 0, unroll=4)


def tail_kernel(inner, from_pair, from_next, w_head, tissue, owners, out, edge, shown):
    depth = 4
    height, lanes = inner.shape[2:]
    rows = inner.shape[1] - 2
    cu = from_pair.shape[0] // rows
    odd, _, _ = neighbours()
    a = from_pair[...].astype(F32)
    b = from_next[...].astype(F32)
    edge[0] = jnp.where(odd == 1, a, b)
    edge[1] = jnp.where(odd == 1, b, a)
    head = w_head[...]
    gap = jnp.zeros((height - cu, lanes), F32)
    run = 8
    for y0 in range(0, rows, run):
        columns = []
        for y in range(y0, y0 + run):
            parts = []
            value = jnp.concatenate(
                [
                    inner[q, y + 1]
                    + jnp.concatenate([edge[q, y * cu : (y + 1) * cu], gap], axis=0)
                    for q in range(2)
                ],
                axis=0,
            )
            value = jnp.maximum(value, 0.0)
            for _ in range(3):
                part = value.astype(BF16)
                parts.append(part)
                value = value - part.astype(F32)
            columns.append(jnp.concatenate(parts, axis=0))
        logits = jnp.dot(head, jnp.concatenate(columns, axis=1), preferred_element_type=F32)
        chance = jax.nn.sigmoid(logits)
        for j in range(run):
            shown[(y0 + j) * 24 : (y0 + j) * 24 + 16] = chance[:, j * lanes : (j + 1) * lanes]

    sub = iota((BY, lanes), 0)
    group = iota((BY, lanes), 1) // BX
    faces = 3 * depth
    tiles = []
    for f in range(faces):
        blocks = []
        line = f % depth * 3 + f // depth
        for by in range(rows // BY):
            v = shown[pl.ds(by * BY * 24 + line, BY, stride=24), :]
            for k in (1, 2, 4):
                s_bit = (sub // k) % 2
                g_bit = (group // k) % 2
                down = pltpu.roll(pltpu.roll(v, BY - k, 0), k * BX, 1)
                up = pltpu.roll(pltpu.roll(v, k, 0), lanes - k * BX, 1)
                v = jnp.where(s_bit == g_bit, v, jnp.where(s_bit < g_bit, down, up))
            blocks.append(v)
        tiles.append(jnp.concatenate(blocks, axis=0))
    tiles = jnp.concatenate(tiles, axis=1).astype(BF16)

    count = tissue.shape[1]
    slots = out.shape[0]
    own = jnp.broadcast_to(owners[...], (count, count))
    seen = jnp.broadcast_to(tissue[...], (count, count))
    r = iota((count, count), 0)
    c = iota((count, count), 1)
    own_column = jnp.sum(jnp.where(r == c, own, 0), axis=1, keepdims=True)
    seen_column = jnp.sum(jnp.where(r == c, seen, 0), axis=1, keepdims=True)
    before = jnp.where(jnp.logical_and(own_column == own, r < c), 1, 0)
    slot = owners[...] * SEND_CAP + jnp.sum(before, axis=0, keepdims=True)
    slot_pick = (iota((slots, count), 0) == slot).astype(F32).astype(BF16)
    blocks = tiles.shape[0]
    block_pick = (seen_column == iota((count, blocks), 1)).astype(F32).astype(BF16)
    select = jnp.dot(slot_pick, block_pick, preferred_element_type=F32).astype(BF16)
    out[...] = jnp.dot(select, tiles, preferred_element_type=F32).astype(BF16)


def on_device(features, w_first, w_second, w_lift, w_merge, w_affine, tissue, owners):
    c0, depth, rows, lanes = features.shape
    c1, c2 = w_lift.shape
    cu = w_merge.shape[0]
    devices = lax.axis_size("gz")
    pair = [(i, i ^ 1) for i in range(devices)]
    after = [(i, i + 1) for i in range(1, devices - 1, 2)]
    after = after + [(j, i) for i, j in after]

    def swap(to_pair, to_next):
        from_next = lax.ppermute(to_next, "gz", after)
        from_pair = lax.ppermute(to_pair, "gz", pair)
        return from_pair, from_next

    vmem = pl.BlockSpec(memory_space=pltpu.VMEM)
    shape = jax.ShapeDtypeStruct
    pitch = rows + 8
    group = 4 * c0

    def call(kernel, outs, count, scratch, mib, flops, space=vmem):
        return pl.pallas_call(
            kernel,
            out_shape=outs,
            in_specs=[space] * count,
            out_specs=jax.tree.map(lambda _: vmem, outs),
            scratch_shapes=scratch,
            compiler_params=pltpu.CompilerParams(vmem_limit_bytes=mib * 2**20),
            cost_estimate=pl.CostEstimate(
                flops=flops, bytes_accessed=4 * 2**20, transcendentals=0
            ),
        )

    halo = shape((c0, HALO, rows, lanes), BF16)
    sources = (features, w_first, w_merge, w_affine, w_second, w_lift)
    to_pair, to_next, *held = call(
        cut_kernel,
        tuple(pltpu.VMEM(a.shape, a.dtype) for a in (halo, halo, *sources)),
        len(sources),
        [pltpu.SemaphoreType.DMA((2 + len(sources),))],
        60,
        0,
        pl.BlockSpec(memory_space=pltpu.HBM),
    )(*sources)
    features, w_first, w_merge, w_affine, w_second, w_lift = held
    from_pair, from_next = swap(to_pair, to_next)

    tops = shape((rows // 4, c1, lanes), BF16)
    taps, near, tops_to_pair, tops_to_next = call(
        local_kernel,
        (shape((2 * c1, 9 * group), BF16), shape((2, rows, c1, lanes), BF16), tops, tops),
        2,
        [
            pltpu.VMEM((group * pitch, lanes), F32),
            pltpu.VMEM((rows + 2, 3 * group, lanes), BF16),
        ],
        12,
        2 * 27 * c0 * c1 * 2 * rows * lanes,
    )(w_first, features)
    tops_pair, tops_next = swap(tops_to_pair, tops_to_next)

    first = call(
        first_kernel,
        shape((4, rows, c1, lanes), BF16),
        4,
        [
            pltpu.VMEM((2, group * pitch, lanes), F32),
            pltpu.VMEM((2, rows + 2, 3 * group, lanes), BF16),
        ],
        12,
        2 * 27 * c0 * c1 * 4 * rows * lanes,
    )(taps, features, from_pair, from_next)
    w_edge, w_inner, head = call(
        weights_kernel,
        (
            shape((6 * cu, 6 * c1), BF16),
            shape((2, 6 * cu, 9 * c1), BF16),
            shape((16, 12 * cu), BF16),
        ),
        2,
        [],
        4,
        2**20,
    )(w_merge, w_affine)
    edges = shape((rows * cu, lanes), BF16)
    to_pair, to_next, cols_3 = call(
        trunk_kernel,
        (edges, edges, shape((depth, rows, 3 * c1, lanes), BF16)),
        7,
        [
            pltpu.VMEM((3, rows // 2 + 2, 3 * c1, lanes), BF16),
            pltpu.VMEM((rows + 2, 2 * cu, lanes), F32),
            pltpu.VMEM((rows * cu, lanes), F32),
        ],
        16,
        2 * 27 * c1 * c2 * depth * rows * lanes // 8,
    )(first, near, tops_pair, tops_next, w_second, w_lift, w_edge)
    edge_pair, edge_next = swap(to_pair, to_next)
    inner = call(
        inner_kernel,
        shape((2, rows + 2, 2 * cu, lanes), F32),
        2,
        [],
        16,
        2 * 27 * c1 * cu * depth * rows * lanes,
    )(cols_3, w_inner)
    outgoing = call(
        tail_kernel,
        shape((devices * SEND_CAP, 3 * depth * BY * BX), BF16),
        6,
        [
            pltpu.VMEM((2, rows * cu, lanes), F32),
            pltpu.VMEM((rows * 24, lanes), F32),
        ],
        8,
        2**20,
    )(inner, edge_pair, edge_next, head, tissue, owners)
    outgoing = outgoing.reshape(devices, SEND_CAP, -1)
    return lax.all_to_all(outgoing, "gz", split_axis=0, concat_axis=0, tiled=True)[None]


def solution(mesh):
    placed = (
        P(None, ("grp", "gz"), None, None),
        P(),
        P(),
        P(),
        P(),
        P(),
        P(("grp", "gz"), None),
        P(("grp", "gz"), None),
    )
    return jax.shard_map(
        on_device,
        mesh=mesh,
        in_specs=placed,
        out_specs=P(("grp", "gz"), None, None, None),
        check_vma=False,
    )
```

```python
import jax
import jax.numpy as jnp
from jax import lax
from jax.experimental import pallas as pl
from jax.experimental.pallas import tpu as pltpu
from jax.sharding import PartitionSpec as P


BY = 8
BX = 16
SEND_CAP = 2
HALO = 2
F32 = jnp.float32
BF16 = jnp.bfloat16


def iota(shape, dim):
    return lax.broadcasted_iota(jnp.int32, shape, dim)


def beside(value, width):
    lane = iota(value.shape, 1) % width
    left = jnp.where(lane == 0, jnp.zeros_like(value), pltpu.roll(value, 1, 1))
    right = jnp.where(
        lane == width - 1, jnp.zeros_like(value), pltpu.roll(value, value.shape[1] - 1, 1)
    )
    return left, value, right


def neighbours():
    here = lax.axis_index("gz")
    return here % 2, here > 0, here < lax.axis_size("gz") - 1


def cut_kernel(features, *rest):
    *refs, sems = rest
    half = (len(refs) - 2) // 2
    weights, (to_next, held), fetched = refs[:half], refs[half : half + 2], refs[half + 2 :]
    odd = lax.axis_index("gz") % 2
    at = jnp.where(odd == 1, features.shape[1] - HALO, 0)
    pairs = zip((features.at[:, pl.ds(at, HALO)], features, *weights), (to_next, held, *fetched))
    copies = [pltpu.make_async_copy(*pair, sems.at[k]) for k, pair in enumerate(pairs)]
    for copy in copies:
        copy.start()
    for copy in copies:
        copy.wait()


def spread(plain, cols, pitch, group, rows):
    blank = jnp.zeros((3 * group, plain.shape[1]), BF16)
    cols[0] = blank
    cols[rows + 1] = blank
    for y in range(rows):
        face = plain[pl.ds(y, group, stride=pitch), :].astype(BF16)
        cols[y + 1] = jnp.concatenate(beside(face, face.shape[1]), axis=0)


def convolve_pair(weight, cols, first, at, rows, c1):
    run = 16
    lanes = cols.shape[2]
    for y in range(0, rows, run):
        x = jnp.concatenate(
            [
                jnp.concatenate([cols[y + b + j] for b in range(3)], axis=0)
                for j in range(run)
            ],
            axis=1,
        )
        out = jnp.dot(weight, x, preferred_element_type=F32)
        out = jnp.maximum(out, 0.0).astype(BF16)
        for j in range(run):
            for z in range(2):
                first[at + z, y + j] = out[z * c1 : (z + 1) * c1, j * lanes : (j + 1) * lanes]


def crest(*faces):
    top = faces[0]
    for face in faces[1:]:
        top = jnp.maximum(top, face)
    return jnp.maximum(top, pltpu.roll(top, top.shape[1] - 1, 1))


def even_lanes(lanes):
    return (iota((2 * lanes, lanes), 0) == 2 * iota((2 * lanes, lanes), 1)).astype(BF16)


def local_kernel(w_first, features, taps, near, to_pair, to_next, plain, cols):
    c0, depth, rows, lanes = features.shape
    c1 = w_first.shape[0]
    odd, _, _ = neighbours()
    pitch = plain.shape[0] // (depth * c0)
    weight = w_first[...]
    blank = jnp.zeros((c1, c0), BF16)
    for o in range(2):
        line = []
        for b in range(3):
            for d in range(3):
                for z in range(4):
                    at = (((z - o) * 3 + b) * 3 + d) * c0
                    line.append(weight[:, at : at + c0] if 0 <= z - o < 3 else blank)
        taps[o * c1 : (o + 1) * c1] = jnp.concatenate(line, axis=1)
    for z in range(depth):
        for c in range(c0):
            at = (z * c0 + c) * pitch
            plain[at : at + rows] = features[c, z].astype(F32)
    spread(plain, cols, pitch, 4 * c0, rows)
    convolve_pair(taps[...], cols, near, 0, rows, c1)
    fold = rows // 4
    base = HALO * c0 * rows
    for z in range(HALO):
        for c in range(c0):
            at = (z * c0 + c) * rows
            to_pair[at : at + rows] = features[c, jnp.where(odd == 1, 0, depth - HALO) + z]
    tops = []
    for z in range(2):
        for y in range(fold):
            tops.append(
                jnp.concatenate(
                    [
                        crest(near[z, 2 * k], near[z, 2 * k + 1])
                        for k in (y, y + fold)
                    ],
                    axis=1,
                )
            )
    packed = jnp.dot(
        jnp.concatenate(tops, axis=0), even_lanes(lanes), preferred_element_type=F32
    ).astype(BF16)
    for y in range(fold):
        down = packed[y * c1 : (y + 1) * c1]
        up = packed[(fold + y) * c1 : (fold + y + 1) * c1]
        to_pair[base + y * c1 : base + (y + 1) * c1] = jnp.where(odd == 1, down, up)
        to_next[y] = jnp.where(odd == 1, up, down)


def first_kernel(taps, features, from_pair, from_next, first, plain, cols):
    c0, depth, rows, _ = features.shape
    c1 = first.shape[2]
    odd, _, _ = neighbours()
    pitch = plain.shape[1] // (4 * c0)
    for z in range(2):
        for c in range(c0):
            at = (z * c0 + c) * pitch
            after = ((z + 2) * c0 + c) * pitch
            k = (z * c0 + c) * rows
            a = from_pair[k : k + rows].astype(F32)
            b = from_next[c, z].astype(F32)
            plain[0, at : at + rows] = jnp.where(odd == 1, a, b)
            plain[1, after : after + rows] = jnp.where(odd == 1, b, a)
            plain[0, after : after + rows] = features[c, z].astype(F32)
            plain[1, at : at + rows] = features[c, depth - 2 + z].astype(F32)
    weight = taps[...]
    for g in range(2):
        spread(plain.at[g], cols.at[g], pitch, 4 * c0, rows)
        convolve_pair(weight, cols.at[g], first, 2 * g, rows, c1)


def trunk_kernel(
    first,
    near,
    from_pair,
    from_next,
    w_second,
    w_lift,
    w_edge,
    to_pair,
    to_next,
    cols_3,
    cols_2,
    border,
    edge,
):
    _, rows, c1, lanes = first.shape
    c2 = w_second.shape[0]
    depth = cols_3.shape[0]
    half_rows = rows // 2
    odd, low_ok, high_ok = neighbours()
    own = (first.at[1], near.at[0], near.at[1], first.at[2])

    pick = even_lanes(lanes)
    lane = iota((c1, lanes), 1)
    low_half = lane < lanes // 2
    keep_low = jnp.logical_or(jnp.logical_not(low_half), low_ok)
    keep_high = jnp.logical_or(low_half, high_ok)
    pad_2 = jnp.zeros((3 * c1, lanes), BF16)
    zero_2 = jnp.zeros((c1, lanes), BF16)
    for a in range(3):
        cols_2[a, 0] = pad_2
        cols_2[a, half_rows + 1] = pad_2
    run_p = 4
    fold = half_rows // 2
    base = from_pair.shape[0] - fold * c1
    for y0 in range(0, half_rows, run_p):
        both = []
        for k in range(y0, y0 + run_p):
            y = 2 * k
            both.append(
                jnp.concatenate(
                    [
                        crest(first[0, y], first[0, y + 1]),
                        crest(own[0][y], own[0][y + 1], own[1][y], own[1][y + 1]),
                    ],
                    axis=1,
                )
            )
            both.append(
                jnp.concatenate(
                    [
                        crest(own[2][y], own[2][y + 1], own[3][y], own[3][y + 1]),
                        crest(first[3, y], first[3, y + 1]),
                    ],
                    axis=1,
                )
            )
        packed = jnp.dot(
            jnp.concatenate(both, axis=0), pick, preferred_element_type=F32
        ).astype(BF16)
        for j in range(run_p):
            k = y0 + j
            at = 2 * j * c1
            a = from_pair[base + k % fold * c1 : base + (k % fold + 1) * c1]
            b = from_next[k % fold]
            below = jnp.where(odd == 1, a, b)
            above = jnp.where(odd == 1, b, a)
            if k < fold:
                above = pltpu.roll(above, lanes // 2, 1)
            else:
                below = pltpu.roll(below, lanes // 2, 1)
            low = packed[at : at + c1]
            high = packed[at + c1 : at + 2 * c1]
            low = jnp.where(low_half, jnp.maximum(low, below), low)
            high = jnp.where(low_half, high, jnp.maximum(high, above))
            low = jnp.where(keep_low, low, zero_2)
            high = jnp.where(keep_high, high, zero_2)
            middle = pltpu.roll(jnp.where(low_half, high, low), lanes // 2, 1)
            for a, value in enumerate((low, middle, high)):
                cols_2[a, k + 1] = jnp.concatenate(beside(value, lanes // 2), axis=0)

    weight_2 = w_second[...]
    weight_l = w_lift[...]
    widen = (iota((lanes, 2 * lanes), 0) == iota((lanes, 2 * lanes), 1) // 2).astype(BF16)
    run_2 = 8

    def conv_2(i, carry):
        y = i * run_2
        x = jnp.concatenate(
            [
                jnp.concatenate(
                    [cols_2[a, y + b + j] for a in range(3) for b in range(3)], axis=0
                )
                for j in range(run_2)
            ],
            axis=1,
        )
        second = jnp.dot(weight_2, x, preferred_element_type=F32)
        second = jnp.maximum(second, 0.0).astype(BF16)
        stacked = jnp.concatenate(
            [second[:, j * lanes : (j + 1) * lanes] for j in range(run_2)], axis=0
        )
        stacked = jnp.dot(stacked, widen, preferred_element_type=F32).astype(BF16)
        spread = jnp.concatenate(
            [stacked[j * c2 : (j + 1) * c2] for j in range(run_2)], axis=1
        )
        lifted = jnp.dot(weight_l, spread, preferred_element_type=F32)
        for j in range(run_2):
            for zz in range(2):
                at = (2 * j + zz) * lanes
                value = lifted[:, at : at + lanes]
                for dz in range(2):
                    for dy in range(2):
                        z = 2 * zz + dz
                        row = 2 * (y + j) + dy
                        merged = value + own[z][row].astype(F32)
                        merged = merged.astype(BF16)
                        cols_3[z, row] = jnp.concatenate(beside(merged, lanes), axis=0)
        return carry

    lax.fori_loop(0, half_rows // run_2, conv_2, 0, unroll=2)

    cu = edge.shape[0] // rows
    border[...] = jnp.zeros_like(border)
    weight_e = w_edge[...]
    run_e = 8

    def conv_e(i, carry):
        y = i * run_e
        x = jnp.concatenate(
            [
                jnp.concatenate([cols_3[0, y + j], cols_3[depth - 1, y + j]], axis=0)
                for j in range(run_e)
            ],
            axis=1,
        )
        out = jnp.dot(weight_e, x, preferred_element_type=F32)
        for k, term in row_sums(out, run_e, 2 * cu, lanes):
            border[y + k] += term
        return carry

    lax.fori_loop(0, rows // run_e, conv_e, 0, unroll=4)

    for target, upward in ((to_pair, odd == 0), (to_next, odd == 1)):
        for y in range(rows):
            down = border[y + 1, 0:cu]
            up = border[y + 1, cu : 2 * cu]
            edge[y * cu : (y + 1) * cu] = jnp.where(upward, up, down)
        target[...] = edge[...].astype(BF16)


def weights_kernel(w_merge, w_affine, w_edge, w_inner, head):
    cu, width = w_merge.shape
    width = width // 9
    merge = w_merge[...].astype(F32)
    none = jnp.zeros((cu, width), F32)

    def arrange(table):
        lines = []
        for b in range(3):
            for line in table:
                pieces = [
                    none if a is None else merge[:, (a * 3 + b) * width : (a * 3 + b + 1) * width]
                    for a in line
                ]
                lines.append(jnp.concatenate(pieces, axis=1))
        return jnp.concatenate(lines, axis=0).astype(BF16)

    w_edge[...] = arrange([[2, None], [None, 0]])
    w_inner[0] = arrange([[1, 2, None], [0, 1, 2]])
    w_inner[1] = arrange([[None, 0, 1], [0, 1, 2]])

    affine = w_affine[...].astype(F32)
    blank = jnp.zeros_like(affine)
    lines = []
    for z in range(4):
        at = (0, 1, 3, 2).index(z)
        line = [affine if k == at else blank for k in range(4)]
        lines.append(jnp.concatenate(line * 3, axis=1))
    lines.append(jnp.zeros((16 - 4 * affine.shape[0], 12 * cu), F32))
    head[...] = jnp.concatenate(lines, axis=0).astype(BF16)


def row_sums(out, run, height, lanes):
    for k in range(run + 2):
        term = None
        for b in range(3):
            j = k - 2 + b
            if 0 <= j < run:
                value = out[b * height : (b + 1) * height, j * lanes : (j + 1) * lanes]
                term = value if term is None else term + value
        yield k, term


def inner_kernel(cols_3, w_inner, inner):
    _, rows, _, lanes = cols_3.shape
    height = inner.shape[2]
    run = 8
    for q in range(2):
        inner[q, 0] = jnp.zeros((height, lanes), F32)
        inner[q, 1] = jnp.zeros((height, lanes), F32)
        weight = w_inner[q]

        def conv_3(i, carry, q=q, weight=weight):
            y = i * run
            x = jnp.concatenate(
                [
                    jnp.concatenate([cols_3[q + a, y + j] for a in range(3)], axis=0)
                    for j in range(run)
                ],
                axis=1,
            )
            out = jnp.dot(weight, x, preferred_element_type=F32)
            for k, term in row_sums(out, run, height, lanes):
                if k < 2:
                    inner[q, y + k] += term
                else:
                    inner[q, y + k] = term
            return carry

        lax.fori_loop(0, rows // run, conv_3, 0, unroll=4)


def tail_kernel(inner, from_pair, from_next, w_head, tissue, owners, out, edge, shown):
    depth = 4
    height, lanes = inner.shape[2:]
    rows = inner.shape[1] - 2
    cu = from_pair.shape[0] // rows
    odd, _, _ = neighbours()
    a = from_pair[...].astype(F32)
    b = from_next[...].astype(F32)
    edge[0] = jnp.where(odd == 1, a, b)
    edge[1] = jnp.where(odd == 1, b, a)
    head = w_head[...]
    gap = jnp.zeros((height - cu, lanes), F32)
    run = 8
    for y0 in range(0, rows, run):
        columns = []
        for y in range(y0, y0 + run):
            parts = []
            value = jnp.concatenate(
                [
                    inner[q, y + 1]
                    + jnp.concatenate([edge[q, y * cu : (y + 1) * cu], gap], axis=0)
                    for q in range(2)
                ],
                axis=0,
            )
            value = jnp.maximum(value, 0.0)
            for _ in range(3):
                part = value.astype(BF16)
                parts.append(part)
                value = value - part.astype(F32)
            columns.append(jnp.concatenate(parts, axis=0))
        logits = jnp.dot(head, jnp.concatenate(columns, axis=1), preferred_element_type=F32)
        chance = jax.nn.sigmoid(logits)
        for j in range(run):
            shown[(y0 + j) * 24 : (y0 + j) * 24 + 16] = chance[:, j * lanes : (j + 1) * lanes]

    sub = iota((BY, lanes), 0)
    group = iota((BY, lanes), 1) // BX
    faces = 3 * depth
    tiles = []
    for f in range(faces):
        blocks = []
        line = f % depth * 3 + f // depth
        for by in range(rows // BY):
            v = shown[pl.ds(by * BY * 24 + line, BY, stride=24), :]
            for k in (1, 2, 4):
                s_bit = (sub // k) % 2
                g_bit = (group // k) % 2
                down = pltpu.roll(pltpu.roll(v, BY - k, 0), k * BX, 1)
                up = pltpu.roll(pltpu.roll(v, k, 0), lanes - k * BX, 1)
                v = jnp.where(s_bit == g_bit, v, jnp.where(s_bit < g_bit, down, up))
            blocks.append(v)
        tiles.append(jnp.concatenate(blocks, axis=0))
    tiles = jnp.concatenate(tiles, axis=1).astype(BF16)

    count = tissue.shape[1]
    slots = out.shape[0]
    own = jnp.broadcast_to(owners[...], (count, count))
    seen = jnp.broadcast_to(tissue[...], (count, count))
    r = iota((count, count), 0)
    c = iota((count, count), 1)
    own_column = jnp.sum(jnp.where(r == c, own, 0), axis=1, keepdims=True)
    seen_column = jnp.sum(jnp.where(r == c, seen, 0), axis=1, keepdims=True)
    before = jnp.where(jnp.logical_and(own_column == own, r < c), 1, 0)
    slot = owners[...] * SEND_CAP + jnp.sum(before, axis=0, keepdims=True)
    slot_pick = (iota((slots, count), 0) == slot).astype(F32).astype(BF16)
    blocks = tiles.shape[0]
    block_pick = (seen_column == iota((count, blocks), 1)).astype(F32).astype(BF16)
    select = jnp.dot(slot_pick, block_pick, preferred_element_type=F32).astype(BF16)
    out[...] = jnp.dot(select, tiles, preferred_element_type=F32).astype(BF16)


def on_device(features, w_first, w_second, w_lift, w_merge, w_affine, tissue, owners):
    c0, depth, rows, lanes = features.shape
    c1, c2 = w_lift.shape
    cu = w_merge.shape[0]
    devices = lax.axis_size("gz")
    pair = [(i, i ^ 1) for i in range(devices)]
    after = [(i, i + 1) for i in range(1, devices - 1, 2)]
    after = after + [(j, i) for i, j in after]

    def swap(value, partners):
        return lax.ppermute(value, "gz", partners)

    vmem = pl.BlockSpec(memory_space=pltpu.VMEM)
    shape = jax.ShapeDtypeStruct
    pitch = rows + 8
    group = 4 * c0

    def call(kernel, outs, count, scratch, mib, flops, space=vmem):
        return pl.pallas_call(
            kernel,
            out_shape=outs,
            in_specs=[space] * count,
            out_specs=jax.tree.map(lambda _: vmem, outs),
            scratch_shapes=scratch,
            compiler_params=pltpu.CompilerParams(vmem_limit_bytes=mib * 2**20),
            cost_estimate=pl.CostEstimate(
                flops=flops, bytes_accessed=4 * 2**20, transcendentals=0
            ),
        )

    halo = shape((c0, HALO, rows, lanes), BF16)
    sources = (features, w_first, w_merge, w_affine, w_second, w_lift)
    to_next, *held = call(
        cut_kernel,
        tuple(pltpu.VMEM(a.shape, a.dtype) for a in (halo, *sources)),
        len(sources),
        [pltpu.SemaphoreType.DMA((1 + len(sources),))],
        60,
        0,
        pl.BlockSpec(memory_space=pltpu.HBM),
    )(*sources)
    features, w_first, w_merge, w_affine, w_second, w_lift = held
    from_next = swap(to_next, after)

    tops = shape((rows // 4, c1, lanes), BF16)
    both = shape((HALO * c0 * rows + rows // 4 * c1, lanes), BF16)
    taps, near, to_pair, tops_to_next = call(
        local_kernel,
        (shape((2 * c1, 9 * group), BF16), shape((2, rows, c1, lanes), BF16), both, tops),
        2,
        [
            pltpu.VMEM((group * pitch, lanes), F32),
            pltpu.VMEM((rows + 2, 3 * group, lanes), BF16),
        ],
        12,
        2 * 27 * c0 * c1 * 2 * rows * lanes,
    )(w_first, features)
    tops_next = swap(tops_to_next, after)
    from_pair = swap(to_pair, pair)

    first = call(
        first_kernel,
        shape((4, rows, c1, lanes), BF16),
        4,
        [
            pltpu.VMEM((2, group * pitch, lanes), F32),
            pltpu.VMEM((2, rows + 2, 3 * group, lanes), BF16),
        ],
        12,
        2 * 27 * c0 * c1 * 4 * rows * lanes,
    )(taps, features, from_pair, from_next)
    w_edge, w_inner, head = call(
        weights_kernel,
        (
            shape((6 * cu, 6 * c1), BF16),
            shape((2, 6 * cu, 9 * c1), BF16),
            shape((16, 12 * cu), BF16),
        ),
        2,
        [],
        4,
        2**20,
    )(w_merge, w_affine)
    edges = shape((rows * cu, lanes), BF16)
    to_pair, to_next, cols_3 = call(
        trunk_kernel,
        (edges, edges, shape((depth, rows, 3 * c1, lanes), BF16)),
        7,
        [
            pltpu.VMEM((3, rows // 2 + 2, 3 * c1, lanes), BF16),
            pltpu.VMEM((rows + 2, 2 * cu, lanes), F32),
            pltpu.VMEM((rows * cu, lanes), F32),
        ],
        16,
        2 * 27 * c1 * c2 * depth * rows * lanes // 8,
    )(first, near, from_pair, tops_next, w_second, w_lift, w_edge)
    edge_next = swap(to_next, after)
    edge_pair = swap(to_pair, pair)
    inner = call(
        inner_kernel,
        shape((2, rows + 2, 2 * cu, lanes), F32),
        2,
        [],
        16,
        2 * 27 * c1 * cu * depth * rows * lanes,
    )(cols_3, w_inner)
    outgoing = call(
        tail_kernel,
        shape((devices * SEND_CAP, 3 * depth * BY * BX), BF16),
        6,
        [
            pltpu.VMEM((2, rows * cu, lanes), F32),
            pltpu.VMEM((rows * 24, lanes), F32),
        ],
        8,
        2**20,
    )(inner, edge_pair, edge_next, head, tissue, owners)
    outgoing = outgoing.reshape(devices, SEND_CAP, -1)
    return lax.all_to_all(outgoing, "gz", split_axis=0, concat_axis=0, tiled=True)[None]


def solution(mesh):
    placed = (
        P(None, ("grp", "gz"), None, None),
        P(),
        P(),
        P(),
        P(),
        P(),
        P(("grp", "gz"), None),
        P(("grp", "gz"), None),
    )
    return jax.shard_map(
        on_device,
        mesh=mesh,
        in_specs=placed,
        out_specs=P(("grp", "gz"), None, None, None),
        check_vma=False,
    )
```
